128 devices in a mesh: space: 32 (over z, x, core), rep: 4 (over y).
Axes of the slice: x: 4, y: 4, z: 4, core: 2. Of those that a mesh axis runs over, the one named last changes fastest.
Arguments:
- voxels: bfloat16 [4, 128, 512, 128], P('rep', 'space'), may hold values from -6 to 6
- occupied: int32 [4, 128], P('rep', 'space'), may hold values from 0 to 1, as said below
- neighbours: int32 [4, 128, 6], P('rep', 'space'), may hold values from -1 to 127, as said below
- first_weight: bfloat16 [27, 128, 128], replicated, may hold values from -0.109375 to 0.109375
- second_weight: bfloat16 [27, 128, 128], replicated, may hold values from -0.109375 to 0.109375
- cotangent: bfloat16 [4, 128, 512, 128], P('rep', 'space'), may hold values from -0.01171875 to 0.01171875
Outputs:
- output_field: bfloat16 [4, 128, 512, 128], P('rep', 'space')
- first_grad: float32 [27, 128, 128], replicated
- second_grad: float32 [27, 128, 128], replicated
The draws below stay inside these ranges and needn't reach their ends.
Inputs may be any that keep to these rules, and one draw needn't show every extreme that they name: In every slab each device of space holds n blocks in its first n slots (occupied 1) and padding after them, n from 1 to 4; in some slab the last device holds 4. `neighbours`: device s of space owns one tile of 2 x 2 x 1 block positions. With h = log2(32) - 1, bit h of s is the tile's third coordinate (the slab is two tiles deep in the third dimension), and below it bit 2k of s is bit k of the tile's first coordinate and bit 2k+1 of s bit k of its second. Entry f names owner * 4 + slot of the occupied block of the same slab across face f (-x, +x, -y, +y, -z, +z), or -1 where there is none or the slot is padding; if a names b across face f, b names a across the opposite face.
All inputs are finite; a program needn't handle non-finite values.
Results may differ from the reference program's by a relative error of at most 0.0031.
Values may be sent and summed in bfloat16 or wider, within the bound.
No kernel may reach another device: no remote copies, remote signals or barrier semaphores. Data moves between devices by JAX's collectives and lax.ppermute only.
A program may use at most 128 MiB of HBM per device.

```python
import jax
import jax.numpy as jnp
from jax import lax

C = 128
EDGE = 8
DEPTH = 1
BLK = 4
VOX = 512
OWNERS = 32
REPS = 4
SLOTS = 128


def morton_owner(column, row_pos, layer, bit_total):
    plane_bits = bit_total - 1
    wide_bits = (plane_bits + 1) // 2
    tall_bits = plane_bits // 2
    owner = layer * 2 ** plane_bits
    for bit_place in range(wide_bits):
        owner = owner + column // 2 ** bit_place % 2 * 4 ** bit_place
    for bit_place in range(tall_bits):
        owner = owner + row_pos // 2 ** bit_place % 2 * (2 * 4 ** bit_place)
    return owner


def slab_layout(key):
    base = jax.random.fold_in(key, 17)
    count_key, order_key, full_key = jax.random.split(base, 3)
    counts = jax.random.randint(count_key, (REPS, OWNERS), BLK // 4, BLK + 1)
    full_slab = jax.random.randint(full_key, (), 0, REPS)
    slab_ids = jnp.arange(REPS)[:, None]
    owner_ids = jnp.arange(OWNERS)[None, :]
    counts = jnp.where((slab_ids == full_slab) & (owner_ids == OWNERS - 1), BLK, counts).astype(jnp.int32)
    order_keys = jax.random.split(order_key, REPS * OWNERS)
    placed = jax.vmap(lambda single: jax.random.permutation(single, BLK))(order_keys)
    placed = placed.reshape(REPS, OWNERS, BLK).astype(jnp.int32)
    matches = placed[:, :, :, None] == jnp.arange(BLK)[None, None, None, :]
    slot_of = jnp.sum(matches.astype(jnp.int32) * jnp.arange(BLK, dtype=jnp.int32)[None, None, :, None], axis=2)
    flat_slots = slot_of.reshape(REPS, OWNERS * BLK)
    bit_total = int(OWNERS).bit_length() - 1
    plane_bits = bit_total - 1
    wide_bits = (plane_bits + 1) // 2
    tall_bits = plane_bits // 2
    owner_vec = jnp.arange(OWNERS, dtype=jnp.int32)
    tile_column = jnp.zeros_like(owner_vec)
    tile_row = jnp.zeros_like(owner_vec)
    for bit_place in range(wide_bits):
        tile_column = tile_column + owner_vec // 2 ** (2 * bit_place) % 2 * 2 ** bit_place
    for bit_place in range(tall_bits):
        tile_row = tile_row + owner_vec // 2 ** (2 * bit_place + 1) % 2 * 2 ** bit_place
    tile_layer = owner_vec // 2 ** plane_bits
    columns_total = 2 * 2 ** wide_bits
    rows_total = 2 * 2 ** tall_bits
    layers_total = 2 * DEPTH
    across = placed // (2 * DEPTH)
    along = placed // DEPTH % 2
    height = placed % DEPTH
    global_x = 2 * tile_column[None, :, None] + across
    global_y = 2 * tile_row[None, :, None] + along
    global_z = DEPTH * tile_layer[None, :, None] + height
    occupied_self = jnp.arange(BLK)[None, None, :] < counts[:, :, None]
    links = []
    for step_x, step_y, step_z in ((-1, 0, 0), (1, 0, 0), (0, -1, 0), (0, 1, 0), (0, 0, -1), (0, 0, 1)):
        next_x = global_x + step_x
        next_y = global_y + step_y
        next_z = global_z + step_z
        inside = (next_x >= 0) & (next_x < columns_total) & (next_y >= 0) & (next_y < rows_total) & (next_z >= 0) & (next_z < layers_total)
        next_x = jnp.clip(next_x, 0, columns_total - 1)
        next_y = jnp.clip(next_y, 0, rows_total - 1)
        next_z = jnp.clip(next_z, 0, layers_total - 1)
        owner_next = morton_owner(next_x // 2, next_y // 2, next_z // DEPTH, bit_total)
        position_next = (next_x % 2 * 2 + next_y % 2) * DEPTH + next_z % DEPTH
        slot_next = jnp.take_along_axis(flat_slots, (owner_next * BLK + position_next).reshape(REPS, -1), axis=1)
        slot_next = slot_next.reshape(REPS, OWNERS, BLK)
        count_next = jnp.take_along_axis(counts, owner_next.reshape(REPS, -1), axis=1).reshape(REPS, OWNERS, BLK)
        alive = inside & occupied_self & (slot_next < count_next)
        links.append(jnp.where(alive, owner_next * BLK + slot_next, -1))
    neighbour_table = jnp.stack(links, axis=-1).reshape(REPS, SLOTS, 6).astype(jnp.int32)
    occupancy = occupied_self.astype(jnp.int32).reshape(REPS, SLOTS)
    return (occupancy, neighbour_table)


def draw_occupied(key, part):
    return slab_layout(key)[0]


def draw_neighbours(key, part):
    return slab_layout(key)[1]


def level_of(rng, shape, cuts, least, top_value):
    level, own = 1.0, jax.random.fold_in(rng, 6)
    for dim, blocks in cuts:
        heights = jnp.exp(jax.random.uniform(jax.random.fold_in(own, dim), (blocks,), jnp.float32, least / len(cuts), top_value / len(cuts)))
        level = level * jnp.repeat(heights, shape[dim] // blocks).reshape([-1 if axis == dim else 1 for axis in range(len(shape))])
    return level


def centred(rng, extent, scale, reach, shards=(), kind=jnp.bfloat16):
    factor_of = level_of(rng, extent, shards, -0.22, 0.18) if shards else 1.0
    drawn = jax.random.normal(rng, extent, jnp.float32) * scale * factor_of
    return jnp.minimum(jnp.maximum(drawn, -reach), reach).astype(kind)


def setup_inputs(seed: int = 0) -> dict:
    key_of = jax.random.split(jax.random.key(seed), 7)
    voxels = centred(key_of[0], (REPS, SLOTS, VOX, C), 1.0, 6.0, ((0, 4), (1, 32)))
    occupied = draw_occupied(jax.random.fold_in(key_of[6], 71), 0)
    neighbours = draw_neighbours(jax.random.fold_in(key_of[6], 71), 0)
    first_weight = centred(key_of[3], (27, C, C), (27 * C) ** -0.5, 0.109375)
    second_weight = centred(key_of[4], (27, C, C), (27 * C) ** -0.5, 0.109375)
    cotangent = centred(key_of[5], (REPS, SLOTS, VOX, C), ((REPS * SLOTS * VOX) ** -0.5), 0.01171875, ((0, 4), (1, 32)))
    return dict(voxels=voxels, occupied=occupied, neighbours=neighbours, first_weight=first_weight, second_weight=second_weight, cotangent=cotangent)


OPPOSITE_FACES = (1, 0, 3, 2, 5, 4)


def face_layers(blocks):
    return jnp.stack([blocks[:, 0], blocks[:, -1], blocks[:, :, 0], blocks[:, :, -1], blocks[:, :, :, 0], blocks[:, :, :, -1]], axis=1)


def assemble(blocks, faces):
    padded = jnp.pad(blocks, ((0, 0), (1, 1), (1, 1), (1, 1), (0, 0)))
    padded = padded.at[:, 0, 1:-1, 1:-1].set(faces[:, 0])
    padded = padded.at[:, -1, 1:-1, 1:-1].set(faces[:, 1])
    padded = padded.at[:, 1:-1, 0, 1:-1].set(faces[:, 2])
    padded = padded.at[:, 1:-1, -1, 1:-1].set(faces[:, 3])
    padded = padded.at[:, 1:-1, 1:-1, 0].set(faces[:, 4])
    padded = padded.at[:, 1:-1, 1:-1, -1].set(faces[:, 5])
    return padded


def gather_faces(blocks, links):
    slot_count = blocks.shape[0]
    layers = face_layers(blocks).reshape(slot_count * 6, EDGE, EDGE, C)
    valid = links >= 0
    opposite = jnp.array(OPPOSITE_FACES, jnp.int32)
    rows = jnp.where(valid, links * 6 + opposite[None, :], 0).astype(jnp.int32)
    return layers[rows] * valid.astype(blocks.dtype)[:, :, None, None, None]


def tap_group(padded, first_tap, backward):
    columns = []
    for second_tap in range(3):
        for third_tap in range(3):
            if backward:
                starts = (2 - first_tap, 2 - second_tap, 2 - third_tap)
            else:
                starts = (first_tap, second_tap, third_tap)
            piece = padded[:, starts[0]:starts[0] + EDGE, starts[1]:starts[1] + EDGE, starts[2]:starts[2] + EDGE]
            columns.append(piece.reshape(-1, C))
    return jnp.concatenate(columns, axis=1)


def convolve(padded, weights):
    total = jnp.zeros((padded.shape[0] * VOX, C), jnp.float32)
    for first_tap in range(3):
        group = tap_group(padded, first_tap, False)
        stacked = weights[first_tap * 9:(first_tap + 1) * 9].reshape(9 * C, C)
        total = total + jnp.dot(group, stacked, preferred_element_type=jnp.float32)
    return total


def convolve_back(padded, weights):
    total = jnp.zeros((padded.shape[0] * VOX, C), jnp.float32)
    for first_tap in range(3):
        group = tap_group(padded, first_tap, True)
        stacked = jnp.swapaxes(weights[first_tap * 9:(first_tap + 1) * 9], 1, 2).reshape(9 * C, C)
        total = total + jnp.dot(group, stacked, preferred_element_type=jnp.float32)
    return total


def weight_terms(padded, grads):
    parts = []
    for first_tap in range(3):
        group = tap_group(padded, first_tap, False)
        part = lax.dot_general(group, grads, (((0,), (0,)), ((), ())), preferred_element_type=jnp.float32)
        parts.append(part.reshape(9, C, C))
    return jnp.concatenate(parts, axis=0)


def reference(voxels, occupied, neighbours, first_weight, second_weight, cotangent):
    def one_slab(items):
        field, flags, links, incoming = items
        keep = flags.astype(jnp.bfloat16)[:, None, None]
        masked = field * keep
        voxel_mask = jnp.repeat(flags.astype(jnp.float32), VOX)[:, None]
        blocks = masked.reshape(-1, EDGE, EDGE, EDGE, C)
        input_padded = assemble(blocks, gather_faces(blocks, links))
        first = convolve(input_padded, first_weight)
        hidden = (jax.nn.silu(first) * voxel_mask).astype(jnp.bfloat16)
        hidden_blocks = hidden.reshape(-1, EDGE, EDGE, EDGE, C)
        hidden_padded = assemble(hidden_blocks, gather_faces(hidden_blocks, links))
        second = convolve(hidden_padded, second_weight)
        output = ((masked.reshape(-1, C).astype(jnp.float32) + second) * voxel_mask).astype(jnp.bfloat16)
        grad_out = (incoming * keep).reshape(-1, C)
        second_terms = weight_terms(hidden_padded, grad_out)
        grad_blocks = grad_out.reshape(-1, EDGE, EDGE, EDGE, C)
        grad_padded = assemble(grad_blocks, gather_faces(grad_blocks, links))
        grad_hidden = convolve_back(grad_padded, second_weight)
        sigma = jax.nn.sigmoid(first)
        grad_first = (grad_hidden * sigma * (1.0 + first * (1.0 - sigma)) * voxel_mask).astype(jnp.bfloat16)
        first_terms = weight_terms(input_padded, grad_first)
        return output.reshape(-1, VOX, C), first_terms, second_terms

    output_field, first_terms, second_terms = lax.map(one_slab, (voxels, occupied, neighbours, cotangent))
    return output_field, jnp.sum(first_terms, axis=0), jnp.sum(second_terms, axis=0)
```

```python
import functools

import jax
import jax.numpy as jnp
from jax import lax
from jax.experimental import pallas as pl
from jax.experimental.pallas import tpu as pltpu
from jax.sharding import PartitionSpec as P

BF = jnp.bfloat16
F32 = jnp.float32
VMEM = pl.BlockSpec(memory_space=pltpu.VMEM)
SMEM = pl.BlockSpec(memory_space=pltpu.SMEM)
PARAMS = pltpu.CompilerParams(vmem_limit_bytes=56 << 20)
ROWS = 3456
CHUNK = 56


def tile_of(s):
    return (s & 1) | ((s >> 1) & 2), ((s >> 1) & 1) | ((s >> 2) & 2), s >> 4


def owner_of(a, b, z):
    return (a & 1) | ((b & 1) << 1) | ((a >> 1) << 2) | ((b >> 1) << 3) | (z << 4)


def swaps(kind):
    pairs = []
    for s in range(32):
        a, b, z = tile_of(s)
        if kind == "xe":
            a ^= 1
        elif kind == "ye":
            b ^= 1
        elif kind == "z":
            z ^= 1
        elif kind == "xo":
            if a not in (1, 2):
                continue
            a = 3 - a
        elif kind == "yo":
            if b not in (1, 2):
                continue
            b = 3 - b
        pairs.append((s, owner_of(a, b, z)))
    return pairs


SWAPS = tuple(swaps(kind) for kind in ("xe", "xo", "ye", "yo", "z"))


def exchange(sent):
    return tuple(lax.ppermute(a, "space", pairs) for a, pairs in zip(sent, SWAPS))


def remote_links(links, face, device):
    found = []
    for n in range(4):
        link = links[0, n, face]
        valid = link >= 0
        found.append((link, valid, valid & ((link >> 2) != device)))
    return found


def face_of(x, n, axis, layer):
    if axis == 0:
        return x[n, pl.ds(layer * 64, 64), :]
    if axis == 1:
        return jnp.concatenate([x[n, pl.ds(i * 64 + layer * 8, 8), :] for i in range(8)], axis=0)
    return x[n, pl.ds(layer, 64, stride=8), :]


def pack_faces(fields, links, device, sends):
    bits = (device & 1, (device >> 1) & 1, device >> 4)
    for axis in range(3):
        width = 4 if axis == 2 else 2
        for odd in range(1 if axis == 2 else 2):
            send = sends[2 * axis + odd]
            side = bits[axis] ^ (1 - odd)
            rank = jnp.int32(0)
            for n in range(4):
                link = links[0, n, 2 * axis + side]
                remote = (link >= 0) & ((link >> 2) != device)
                at = rank

                @pl.when(remote)
                def _():
                    for a, x in enumerate(fields):
                        row = pl.multiple_of((a * width + at) * 64, 64)
                        send[pl.ds(row, 64), :] = face_of(x, n, axis, side * 7).astype(BF)

                rank = rank + remote.astype(jnp.int32)


def take_faces(x, links, device, got, field, faces):
    bits = (device & 1, (device >> 1) & 1, device >> 4)
    for axis in range(3):
        width = 4 if axis == 2 else 2
        for side in range(2):
            found = remote_links(links, 2 * axis + side, device)
            for n in range(4):
                link, valid, remote = found[n]
                slot = link & 3
                rank = jnp.int32(0)
                for q in range(4):
                    if q != n:
                        lower = found[q][2] & ((found[q][0] & 3) < slot)
                        rank = rank + lower.astype(jnp.int32)
                rank = jnp.minimum(jnp.where(remote, rank, 0), width - 1)
                row = pl.ds(pl.multiple_of((field * width + rank) * 64, 64), 64)
                if axis == 2:
                    far = got[4][row, :].astype(F32)
                    value = jnp.where(remote, far, 0.0)
                else:
                    even = (bits[axis] ^ side) == 1
                    far = jnp.where(even, got[2 * axis][row, :], got[2 * axis + 1][row, :])
                    near = face_of(x, jnp.where(valid, slot, 0), axis, 0 if side else 7)
                    value = jnp.where(valid, jnp.where(remote, far.astype(F32), near), 0.0)
                faces[axis][n, side] = value


def build(wide, odd, x, faces):
    k_of = lax.broadcasted_iota(jnp.int32, (10, 8, 128), 1)
    at_low, at_high = k_of == 0, k_of == 7
    none = jnp.zeros((1, 8, 128), F32)

    def block(n, carry):
        for i in range(10):
            if i in (0, 9):
                core = faces[0][n, 0 if i == 0 else 1].reshape(8, 8, 128)
                layers = jnp.concatenate((none, core, none), axis=0)
                low, high = jnp.zeros_like(layers), jnp.zeros_like(layers)
            else:
                at = pl.ds((i - 1) * 8, 8)
                core = x[n, pl.ds((i - 1) * 64, 64), :].reshape(8, 8, 128)
                layers = jnp.concatenate(
                    (faces[1][n, 0, at, :][None], core, faces[1][n, 1, at, :][None]), axis=0
                )
                low, high = (
                    jnp.concatenate(
                        (none, jnp.broadcast_to(faces[2][n, side, at, :][:, None, :], (8, 8, 128)), none),
                        axis=0,
                    )
                    for side in range(2)
                )
            before = jnp.where(at_low, low, pltpu.roll(layers, 1, 1))
            after = jnp.where(at_high, high, pltpu.roll(layers, 7, 1))
            for tk, shifted in enumerate((before, layers, after)):
                wide[tk, n, i] = shifted.reshape(80, 128).astype(BF)
                odd[tk, n, i] = shifted[1:9].reshape(64, 128).astype(BF)
        return carry

    lax.fori_loop(0, 4, block, 0)


def tap(wide, odd, n, i, tj, tk):
    if tj == 1:
        return odd[tk, n, i]
    return wide[tk, n, i, pl.ds(8 * tj, 64), :]


def convolve(wide, odd, pair_weights, n):
    columns = []
    for layer in range(4):
        for tj in range(3):
            for tk in range(3):
                columns.append(
                    jnp.concatenate([tap(wide, odd, n, 2 * p + layer, tj, tk) for p in range(4)], axis=0)
                )
    group = jnp.concatenate(columns, axis=1)
    both = jnp.dot(group, pair_weights[...], preferred_element_type=F32)
    rows = []
    for p in range(4):
        for half in range(2):
            rows.append(both[p * 64 : (p + 1) * 64, half * 128 : (half + 1) * 128])
    return jnp.concatenate(rows, axis=0)


def lay_weights(pair_weights, block_of):
    pair_weights[pl.ds(3456, 1152), pl.ds(0, 128)] = jnp.zeros((1152, 128), BF)
    pair_weights[pl.ds(0, 1152), pl.ds(128, 128)] = jnp.zeros((1152, 128), BF)
    for t in range(27):
        block = block_of(t)
        pair_weights[pl.ds(t * 128, 128), pl.ds(0, 128)] = block
        pair_weights[pl.ds((t + 9) * 128, 128), pl.ds(128, 128)] = block


def weight_terms(wide, odd, turned, put):
    for ti in range(3):
        columns = []
        for tj in range(3):
            for tk in range(3):
                columns.append(
                    jnp.concatenate(
                        [tap(wide, odd, n, i + ti, tj, tk) for n in range(4) for i in range(8)], axis=0
                    )
                )
        total = jnp.dot(turned[...], jnp.concatenate(columns, axis=1), preferred_element_type=F32)
        for q in range(9):
            put(9 * ti + q, total[:, q * 128 : (q + 1) * 128])


def load_masked(x, source, occupied):
    for n in range(4):
        keep = occupied[0, n].astype(F32)
        x[n] = source[0, n].astype(F32) * keep


def first_faces_kernel(voxels, cotangent, links, occupied, *rest):
    sends, (x, g) = rest[:5], rest[5:]
    device = lax.axis_index("space")
    load_masked(x, voxels, occupied)
    load_masked(g, cotangent, occupied)
    pack_faces((x, g), links, device, sends)


def hidden_faces_kernel(hidden, links, *rest):
    sends, (x,) = rest[:5], rest[5:]
    device = lax.axis_index("space")
    for n in range(4):
        x[n] = hidden[n].astype(F32)
    pack_faces((x,), links, device, sends)


def main_kernel(
    voxels, cotangent, links, occupied, first_weight, second_weight, g0, g1, g2, g3, g4,
    hidden, terms,
    x, fx, fy, fz, wide, odd, wide_grad, odd_grad, pair_weights, slope, hidden_turned, grad_turned,
):
    device = lax.axis_index("space")
    got = (g0, g1, g2, g3, g4)
    faces = (fx, fy, fz)
    load_masked(x, voxels, occupied)
    take_faces(x, links, device, got, 0, faces)
    build(wide, odd, x, faces)
    lay_weights(pair_weights, lambda t: first_weight[t])

    def forward(n, carry):
        keep = occupied[0, n].astype(F32)
        first = convolve(wide, odd, pair_weights, n)
        sigma = jax.nn.sigmoid(first)
        value = (first * sigma * keep).astype(BF)
        hidden[n] = value
        hidden_turned[:, pl.ds(pl.multiple_of(n * 512, 512), 512)] = value.T
        slope[n] = sigma * (1.0 + first * (1.0 - sigma)) * keep
        return carry

    lax.fori_loop(0, 4, forward, 0)

    load_masked(x, cotangent, occupied)
    take_faces(x, links, device, got, 1, faces)
    build(wide_grad, odd_grad, x, faces)
    lay_weights(pair_weights, lambda t: second_weight[26 - t].T)

    def put_second(t, block):
        terms[pl.ds(ROWS + (26 - t) * 128, 128), :] = block.astype(BF)

    weight_terms(wide_grad, odd_grad, hidden_turned, put_second)

    def backward(n, carry):
        grad = convolve(wide_grad, odd_grad, pair_weights, n) * slope[n]
        grad_turned[:, pl.ds(pl.multiple_of(n * 512, 512), 512)] = grad.astype(BF).T
        return carry

    lax.fori_loop(0, 4, backward, 0)

    def put_first(t, block):
        terms[pl.ds(t * 128, 128), :] = block.T.astype(BF)

    weight_terms(wide, odd, grad_turned, put_first)
    terms[pl.ds(2 * ROWS, 256), :] = jnp.zeros((256, 128), BF)


def last_kernel(
    voxels, hidden, links, occupied, second_weight, g0, g1, g2, g3, g4,
    output,
    x, fx, fy, fz, wide, odd, pair_weights,
):
    device = lax.axis_index("space")
    faces = (fx, fy, fz)
    for n in range(4):
        x[n] = hidden[n].astype(F32)
    take_faces(x, links, device, (g0, g1, g2, g3, g4), 0, faces)
    build(wide, odd, x, faces)
    lay_weights(pair_weights, lambda t: second_weight[t])

    def forward(n, carry):
        keep = occupied[0, n].astype(F32)
        second = convolve(wide, odd, pair_weights, n)
        output[0, n] = ((voxels[0, n].astype(F32) * keep + second) * keep).astype(BF)
        return carry

    lax.fori_loop(0, 4, forward, 0)


def sum_kernel(chunks, spread):
    total = chunks[0].astype(F32)

    def add(p, total):
        return total + chunks[p].astype(F32)

    total = lax.fori_loop(1, 128, add, total, unroll=8).astype(BF)

    def put(p, carry):
        spread[p] = total
        return carry

    lax.fori_loop(0, 128, put, 0, unroll=8)


def send_shapes(fields):
    return tuple(jax.ShapeDtypeStruct((fields * w * 64, 128), BF) for w in (2, 2, 2, 2, 4))


def call(kernel, outs, ins, scratch, flops=0, nbytes=0):
    specs = [SMEM if a.dtype == jnp.int32 else VMEM for a in ins]
    many = isinstance(outs, tuple)
    return pl.pallas_call(
        kernel,
        out_shape=outs,
        in_specs=specs,
        out_specs=tuple(VMEM for _ in outs) if many else VMEM,
        scratch_shapes=scratch,
        compiler_params=PARAMS,
        cost_estimate=pl.CostEstimate(flops=flops, bytes_accessed=nbytes, transcendentals=0),
    )(*ins)


def local(voxels, occupied, neighbours, first_weight, second_weight, cotangent):
    field = pltpu.VMEM((4, 512, 128), F32)
    sides = [pltpu.VMEM((4, 2, 64, 128), F32)] * 3
    padded = [pltpu.VMEM((3, 4, 10, 80, 128), BF), pltpu.VMEM((3, 4, 10, 64, 128), BF)]
    pairs = pltpu.VMEM((4608, 256), BF)
    turned = pltpu.VMEM((128, 2048), BF)

    sent = call(
        first_faces_kernel,
        send_shapes(2),
        (voxels, cotangent, neighbours, occupied),
        [field, field],
        nbytes=2 << 20,
    )
    got = exchange(sent)
    hidden, terms = call(
        main_kernel,
        (jax.ShapeDtypeStruct((4, 512, 128), BF), jax.ShapeDtypeStruct((128 * CHUNK, 128), BF)),
        (voxels, cotangent, neighbours, occupied, first_weight, second_weight) + got,
        [field] + sides + padded + padded + [pairs, field, turned, turned],
        flops=8 << 30,
        nbytes=8 << 20,
    )
    parts = lax.all_to_all(
        terms.reshape(128, CHUNK, 128), ("space", "rep"), split_axis=0, concat_axis=0, tiled=True
    )
    sent = call(hidden_faces_kernel, send_shapes(1), (hidden, neighbours), [field], nbytes=1 << 20)
    got = exchange(sent)
    output = call(
        last_kernel,
        jax.ShapeDtypeStruct((1, 4, 512, 128), BF),
        (voxels, hidden, neighbours, occupied, second_weight) + got,
        [field] + sides + padded + [pairs],
        flops=3 << 30,
        nbytes=4 << 20,
    )
    spread = call(
        sum_kernel, jax.ShapeDtypeStruct((128, CHUNK, 128), BF), (parts,), [], nbytes=4 << 20
    )
    whole = lax.all_to_all(spread, ("space", "rep"), split_axis=0, concat_axis=0, tiled=True)
    whole = whole.reshape(128 * CHUNK, 128)
    first_grad = whole[:ROWS].reshape(27, 128, 128).astype(F32)
    second_grad = whole[ROWS : 2 * ROWS].reshape(27, 128, 128).astype(F32)
    return output, first_grad, second_grad


def solution(mesh):
    placed = (
        P("rep", "space", None, None),
        P("rep", "space"),
        P("rep", "space", None),
        P(),
        P(),
        P("rep", "space", None, None),
    )
    return jax.shard_map(
        local,
        mesh=mesh,
        in_specs=placed,
        out_specs=(P("rep", "space", None, None), P(), P()),
        check_vma=False,
    )
```

```python
import functools

import jax
import jax.numpy as jnp
from jax import lax
from jax.experimental import pallas as pl
from jax.experimental.pallas import tpu as pltpu
from jax.sharding import PartitionSpec as P

BF = jnp.bfloat16
F32 = jnp.float32
VMEM = pl.BlockSpec(memory_space=pltpu.VMEM)
SMEM = pl.BlockSpec(memory_space=pltpu.SMEM)
ROWS = 3456
CHUNK = 56


def tile_of(s):
    return (s & 1) | ((s >> 1) & 2), ((s >> 1) & 1) | ((s >> 2) & 2), s >> 4


def owner_of(a, b, z):
    return (a & 1) | ((b & 1) << 1) | ((a >> 1) << 2) | ((b >> 1) << 3) | (z << 4)


def swaps(kind):
    pairs = []
    for s in range(32):
        a, b, z = tile_of(s)
        if kind == "xe":
            a ^= 1
        elif kind == "ye":
            b ^= 1
        elif kind == "z":
            z ^= 1
        elif kind == "xo":
            if a not in (1, 2):
                continue
            a = 3 - a
        elif kind == "yo":
            if b not in (1, 2):
                continue
            b = 3 - b
        pairs.append((s, owner_of(a, b, z)))
    return pairs


SWAPS = tuple(swaps(kind) for kind in ("xe", "xo", "ye", "yo", "z"))


SPACE = ("chip", "core")
PEERS = ("chip", "rep")
PARTNER = ((0, 1), (1, 0))


def exchange(sent):
    return tuple(lax.ppermute(a, SPACE, pairs) for a, pairs in zip(sent, SWAPS))


def remote_links(links, face, device):
    found = []
    for n in range(4):
        link = links[0, n, face]
        valid = link >= 0
        found.append((link, valid, valid & ((link >> 2) != device)))
    return found


def face_of(x, n, axis, layer):
    if axis == 0:
        return x[n, pl.ds(layer * 64, 64), :]
    if axis == 1:
        return jnp.concatenate([x[n, pl.ds(i * 64 + layer * 8, 8), :] for i in range(8)], axis=0)
    return x[n, pl.ds(layer, 64, stride=8), :]


def pack_faces(fields, links, device, sends):
    bits = (device & 1, (device >> 1) & 1, device >> 4)
    for axis in range(3):
        width = 4 if axis == 2 else 2
        for odd in range(1 if axis == 2 else 2):
            send = sends[2 * axis + odd]
            side = bits[axis] ^ (1 - odd)
            rank = jnp.int32(0)
            for n in range(4):
                link = links[0, n, 2 * axis + side]
                remote = (link >= 0) & ((link >> 2) != device)
                at = rank

                @pl.when(remote)
                def _():
                    for a, x in enumerate(fields):
                        row = pl.multiple_of((a * width + at) * 64, 64)
                        send[pl.ds(row, 64), :] = face_of(x, n, axis, side * 7).astype(BF)

                rank = rank + remote.astype(jnp.int32)


def take_faces(x, links, device, got, field, faces):
    bits = (device & 1, (device >> 1) & 1, device >> 4)
    for axis in range(3):
        width = 4 if axis == 2 else 2
        for side in range(2):
            found = remote_links(links, 2 * axis + side, device)
            for n in range(4):
                link, valid, remote = found[n]
                slot = link & 3
                rank = jnp.int32(0)
                for q in range(4):
                    if q != n:
                        lower = found[q][2] & ((found[q][0] & 3) < slot)
                        rank = rank + lower.astype(jnp.int32)
                rank = jnp.minimum(jnp.where(remote, rank, 0), width - 1)
                row = pl.ds(pl.multiple_of((field * width + rank) * 64, 64), 64)
                if axis == 2:
                    far = got[4][row, :].astype(F32)
                    value = jnp.where(remote, far, 0.0)
                else:
                    even = (bits[axis] ^ side) == 1
                    far = jnp.where(even, got[2 * axis][row, :], got[2 * axis + 1][row, :])
                    near = face_of(x, jnp.where(valid, slot, 0), axis, 0 if side else 7)
                    value = jnp.where(valid, jnp.where(remote, far.astype(F32), near), 0.0)
                faces[axis][n, side] = value


def build(wide, odd, x, faces):
    k_of = lax.broadcasted_iota(jnp.int32, (10, 8, 128), 1)
    at_low, at_high = k_of == 0, k_of == 7
    none = jnp.zeros((1, 8, 128), F32)

    def block(n, carry):
        for i in range(10):
            if i in (0, 9):
                core = faces[0][n, 0 if i == 0 else 1].reshape(8, 8, 128)
                layers = jnp.concatenate((none, core, none), axis=0)
                low, high = jnp.zeros_like(layers), jnp.zeros_like(layers)
            else:
                at = pl.ds((i - 1) * 8, 8)
                core = x[n, pl.ds((i - 1) * 64, 64), :].reshape(8, 8, 128)
                layers = jnp.concatenate(
                    (faces[1][n, 0, at, :][None], core, faces[1][n, 1, at, :][None]), axis=0
                )
                low, high = (
                    jnp.concatenate(
                        (none, jnp.broadcast_to(faces[2][n, side, at, :][:, None, :], (8, 8, 128)), none),
                        axis=0,
                    )
                    for side in range(2)
                )
            before = jnp.where(at_low, low, pltpu.roll(layers, 1, 1))
            after = jnp.where(at_high, high, pltpu.roll(layers, 7, 1))
            for tk, shifted in enumerate((before, layers, after)):
                wide[tk, n, i] = shifted.reshape(80, 128).astype(BF)
                odd[tk, n, i] = shifted[1:9].reshape(64, 128).astype(BF)
        return carry

    lax.fori_loop(0, 4, block, 0)


def tap(wide, odd, n, i, tj, tk):
    if tj == 1:
        return odd[tk, n, i]
    return wide[tk, n, i, pl.ds(8 * tj, 64), :]


def convolve(wide, odd, pair_weights, n):
    columns = []
    for layer in range(4):
        for tj in range(3):
            for tk in range(3):
                columns.append(
                    jnp.concatenate([tap(wide, odd, n, 2 * p + layer, tj, tk) for p in range(4)], axis=0)
                )
    group = jnp.concatenate(columns, axis=1)
    both = jnp.dot(group, pair_weights[...], preferred_element_type=F32)
    rows = []
    for p in range(4):
        for half in range(2):
            rows.append(both[p * 64 : (p + 1) * 64, half * 128 : (half + 1) * 128])
    return jnp.concatenate(rows, axis=0)


def lay_weights(pair_weights, block_of):
    pair_weights[pl.ds(3456, 1152), pl.ds(0, 128)] = jnp.zeros((1152, 128), BF)
    pair_weights[pl.ds(0, 1152), pl.ds(128, 128)] = jnp.zeros((1152, 128), BF)
    for t in range(27):
        block = block_of(t)
        pair_weights[pl.ds(t * 128, 128), pl.ds(0, 128)] = block
        pair_weights[pl.ds((t + 9) * 128, 128), pl.ds(128, 128)] = block


def weight_terms(wide, odd, turned, put):
    for ti in range(3):
        columns = []
        for tj in range(3):
            for tk in range(3):
                columns.append(
                    jnp.concatenate(
                        [tap(wide, odd, n, i + ti, tj, tk) for n in range(4) for i in range(8)], axis=0
                    )
                )
        total = jnp.dot(turned[...], jnp.concatenate(columns, axis=1), preferred_element_type=F32)
        for q in range(9):
            put(9 * ti + q, total[:, q * 128 : (q + 1) * 128])


def load_masked(x, source, occupied):
    for n in range(4):
        keep = occupied[0, n].astype(F32)
        x[n] = source[0, n].astype(F32) * keep


def first_faces_kernel(voxels, cotangent, links, occupied, *rest):
    sends, (x, g) = rest[:5], rest[5:]
    device = lax.axis_index(SPACE)
    load_masked(x, voxels, occupied)
    load_masked(g, cotangent, occupied)
    pack_faces((x, g), links, device, sends)


def hidden_faces_kernel(hidden, links, *rest):
    sends, (x,) = rest[:5], rest[5:]
    device = lax.axis_index(SPACE)
    for n in range(4):
        x[n] = hidden[n].astype(F32)
    pack_faces((x,), links, device, sends)


def main_kernel(
    voxels, cotangent, links, occupied, first_weight, second_weight, g0, g1, g2, g3, g4,
    hidden, own_terms, other_terms,
    x, fx, fy, fz, wide, odd, wide_grad, odd_grad, pair_weights, slope, hidden_turned, grad_turned,
):
    device = lax.axis_index(SPACE)
    got = (g0, g1, g2, g3, g4)
    faces = (fx, fy, fz)
    load_masked(x, voxels, occupied)
    take_faces(x, links, device, got, 0, faces)
    build(wide, odd, x, faces)
    lay_weights(pair_weights, lambda t: first_weight[t])

    def forward(n, carry):
        keep = occupied[0, n].astype(F32)
        first = convolve(wide, odd, pair_weights, n)
        sigma = jax.nn.sigmoid(first)
        value = (first * sigma * keep).astype(BF)
        hidden[n] = value
        hidden_turned[:, pl.ds(pl.multiple_of(n * 512, 512), 512)] = value.T
        slope[n] = sigma * (1.0 + first * (1.0 - sigma)) * keep
        return carry

    lax.fori_loop(0, 4, forward, 0)

    load_masked(x, cotangent, occupied)
    take_faces(x, links, device, got, 1, faces)
    build(wide_grad, odd_grad, x, faces)
    lay_weights(pair_weights, lambda t: second_weight[26 - t].T)

    core = device & 1

    def put(of_core, t, block):
        rows = pl.ds(t * 128, 128)

        @pl.when(core == of_core)
        def _():
            own_terms[rows, :] = block

        @pl.when(core != of_core)
        def _():
            other_terms[rows, :] = block

    def put_second(t, block):
        put(1, 26 - t, block)

    weight_terms(wide_grad, odd_grad, hidden_turned, put_second)

    def backward(n, carry):
        grad = convolve(wide_grad, odd_grad, pair_weights, n) * slope[n]
        grad_turned[:, pl.ds(pl.multiple_of(n * 512, 512), 512)] = grad.astype(BF).T
        return carry

    lax.fori_loop(0, 4, backward, 0)

    def put_first(t, block):
        put(0, t, block.T)

    weight_terms(wide, odd, grad_turned, put_first)


def last_kernel(
    voxels, hidden, links, occupied, second_weight, g0, g1, g2, g3, g4,
    output,
    x, fx, fy, fz, wide, odd, pair_weights,
):
    device = lax.axis_index(SPACE)
    faces = (fx, fy, fz)
    for n in range(4):
        x[n] = hidden[n].astype(F32)
    take_faces(x, links, device, (g0, g1, g2, g3, g4), 0, faces)
    build(wide, odd, x, faces)
    lay_weights(pair_weights, lambda t: second_weight[t])

    def forward(n, carry):
        keep = occupied[0, n].astype(F32)
        second = convolve(wide, odd, pair_weights, n)
        output[0, n] = ((voxels[0, n].astype(F32) * keep + second) * keep).astype(BF)
        return carry

    lax.fori_loop(0, 4, forward, 0)


def pair_kernel(own, other, terms):
    terms[pl.ds(0, ROWS), :] = (own[...] + other[...]).astype(BF)
    terms[pl.ds(ROWS, 64 * CHUNK - ROWS), :] = jnp.zeros((64 * CHUNK - ROWS, 128), BF)


def sum_kernel(chunks, *rest):
    spread = rest[-1]
    total = chunks[0].astype(F32)

    def add(p, total):
        return total + chunks[p].astype(F32)

    total = lax.fori_loop(1, 64, add, total, unroll=7).astype(BF)

    def put(p, carry):
        spread[p] = total
        return carry

    lax.fori_loop(0, 64, put, 0, unroll=8)


def finish_kernel(own, other, first_grad, second_grad):
    core = lax.axis_index("core")

    def put(mine, theirs):
        mine[...] = own[pl.ds(0, ROWS), :].astype(F32)
        theirs[...] = other[pl.ds(0, ROWS), :].astype(F32)

    @pl.when(core == 0)
    def _():
        put(first_grad, second_grad)

    @pl.when(core == 1)
    def _():
        put(second_grad, first_grad)


def send_shapes(fields):
    return tuple(jax.ShapeDtypeStruct((fields * w * 64, 128), BF) for w in (2, 2, 2, 2, 4))


def call(kernel, outs, ins, scratch, limit, flops=0, nbytes=0, unread=0):
    specs = [SMEM if a.dtype == jnp.int32 else VMEM for a in ins]
    for at in range(len(ins) - unread, len(ins)):
        specs[at] = pl.BlockSpec(memory_space=pl.ANY)
    many = isinstance(outs, tuple)
    return pl.pallas_call(
        kernel,
        out_shape=outs,
        in_specs=specs,
        out_specs=tuple(VMEM for _ in outs) if many else VMEM,
        scratch_shapes=scratch,
        compiler_params=pltpu.CompilerParams(vmem_limit_bytes=limit << 20),
        cost_estimate=pl.CostEstimate(flops=flops, bytes_accessed=nbytes, transcendentals=0),
    )(*ins)


def local(voxels, occupied, neighbours, first_weight, second_weight, cotangent):
    field = pltpu.VMEM((4, 512, 128), F32)
    sides = [pltpu.VMEM((4, 2, 64, 128), F32)] * 3
    padded = [pltpu.VMEM((3, 4, 10, 80, 128), BF), pltpu.VMEM((3, 4, 10, 64, 128), BF)]
    pairs = pltpu.VMEM((4608, 256), BF)
    turned = pltpu.VMEM((128, 2048), BF)

    sent = call(
        first_faces_kernel,
        send_shapes(2),
        (voxels, cotangent, neighbours, occupied),
        [field, field],
        8,
        nbytes=2 << 20,
    )
    got = exchange(sent)
    terms_shape = jax.ShapeDtypeStruct((ROWS, 128), F32)
    hidden, own, other = call(
        main_kernel,
        (jax.ShapeDtypeStruct((4, 512, 128), BF), terms_shape, terms_shape),
        (voxels, cotangent, neighbours, occupied, first_weight, second_weight) + got,
        [field] + sides + padded + padded + [pairs, field, turned, turned],
        32,
        flops=8 << 30,
        nbytes=8 << 20,
    )
    other = lax.ppermute(other, "core", PARTNER)
    chunks = jax.ShapeDtypeStruct((64 * CHUNK, 128), BF)
    terms = call(pair_kernel, chunks, (own, other), [], 8, nbytes=4 << 20)
    parts = lax.all_to_all(
        terms.reshape(64, CHUNK, 128), PEERS, split_axis=0, concat_axis=0, tiled=True
    )
    sent = call(hidden_faces_kernel, send_shapes(1), (hidden, neighbours), [field], 6, nbytes=1 << 20)
    got = exchange(sent)
    spread = call(
        sum_kernel,
        jax.ShapeDtypeStruct((64, CHUNK, 128), BF),
        (parts,) + got,
        [],
        6,
        nbytes=2 << 20,
        unread=5,
    )
    mine = lax.all_to_all(spread, PEERS, split_axis=0, concat_axis=0, tiled=True)
    output = call(
        last_kernel,
        jax.ShapeDtypeStruct((1, 4, 512, 128), BF),
        (voxels, hidden, neighbours, occupied, second_weight) + got,
        [field] + sides + padded + [pairs],
        20,
        flops=3 << 30,
        nbytes=4 << 20,
    )
    mine, output = lax.optimization_barrier((mine, output))
    mine = mine.reshape(64 * CHUNK, 128)
    theirs = lax.ppermute(mine, "core", PARTNER)
    first_grad, second_grad = call(
        finish_kernel, (terms_shape, terms_shape), (mine, theirs), [], 10, nbytes=6 << 20
    )
    return output, first_grad.reshape(27, 128, 128), second_grad.reshape(27, 128, 128)


def solution(mesh):
    mesh = jax.sharding.Mesh(mesh.devices.reshape(16, 2, 4), ("chip", "core", "rep"))
    placed = (
        P("rep", SPACE, None, None),
        P("rep", SPACE),
        P("rep", SPACE, None),
        P(),
        P(),
        P("rep", SPACE, None, None),
    )
    return jax.shard_map(
        local,
        mesh=mesh,
        in_specs=placed,
        out_specs=(P("rep", SPACE, None, None), P(), P()),
        check_vma=False,
    )
```

```python
import jax
import jax.numpy as jnp
from jax import lax
from jax.experimental import pallas as pl
from jax.experimental.pallas import tpu as pltpu
from jax.sharding import PartitionSpec as P


BF = jnp.bfloat16
F32 = jnp.float32
VMEM = pl.BlockSpec(memory_space=pltpu.VMEM)
HBM = pl.BlockSpec(memory_space=pltpu.HBM)
ANY = pl.BlockSpec(memory_space=pl.ANY)
ROWS = 3456
CHUNK = 56


def tile_of(s):
    return (s & 1) | ((s >> 1) & 2), ((s >> 1) & 1) | ((s >> 2) & 2), s >> 4


def owner_of(a, b, z):
    return (a & 1) | ((b & 1) << 1) | ((a >> 1) << 2) | ((b >> 1) << 3) | (z << 4)


def swaps(kind):
    pairs = []
    for s in range(32):
        a, b, z = tile_of(s)
        if kind == "xe":
            a ^= 1
        elif kind == "ye":
            b ^= 1
        elif kind == "z":
            z ^= 1
        elif kind == "xo":
            if a not in (1, 2):
                continue
            a = 3 - a
        elif kind == "yo":
            if b not in (1, 2):
                continue
            b = 3 - b
        pairs.append((s, owner_of(a, b, z)))
    return pairs


SWAPS = tuple(swaps(kind) for kind in ("xe", "xo", "ye", "yo", "z"))


SPACE = ("chip", "core")
PEERS = ("chip", "rep")
PARTNER = ((0, 1), (1, 0))


def exchange(sent):
    got = []
    for way in range(5):
        got.append(lax.ppermute(sent[way], SPACE, SWAPS[way]))
    return tuple(got)


def remote_links(links, face, device):
    found = []
    for n in range(4):
        link = links[0, n, face]
        valid = link >= 0
        found.append((link, valid, valid & ((link >> 2) != device)))
    return found


def face_of(x, n, axis, layer):
    if axis == 0:
        return x[n, pl.ds(layer * 64, 64), :]
    if axis == 1:
        return jnp.concatenate([x[n, pl.ds(i * 64 + layer * 8, 8), :] for i in range(8)], axis=0)
    return x[n, pl.ds(layer, 64, stride=8), :]


def pack_faces(fields, links, device, sends):
    bits = (device & 1, (device >> 1) & 1, device >> 4)
    for axis in range(3):
        width = 4 if axis == 2 else 2
        for odd in range(1 if axis == 2 else 2):
            send = sends[2 * axis + odd]
            side = bits[axis] ^ (1 - odd)
            rank = jnp.int32(0)
            for n in range(4):
                link = links[0, n, 2 * axis + side]
                remote = (link >= 0) & ((link >> 2) != device)
                at = rank

                @pl.when(remote)
                def _():
                    for a, x in enumerate(fields):
                        row = pl.multiple_of((a * width + at) * 64, 64)
                        send[pl.ds(row, 64), :] = face_of(x, n, axis, side * 7).astype(BF)

                rank = rank + remote.astype(jnp.int32)


def take_faces(x, links, device, got, field, faces):
    bits = (device & 1, (device >> 1) & 1, device >> 4)
    for axis in range(3):
        width = 4 if axis == 2 else 2
        for side in range(2):
            found = remote_links(links, 2 * axis + side, device)
            for n in range(4):
                link, valid, remote = found[n]
                slot = link & 3
                rank = jnp.int32(0)
                for q in range(4):
                    if q != n:
                        lower = found[q][2] & ((found[q][0] & 3) < slot)
                        rank = rank + lower.astype(jnp.int32)
                rank = jnp.minimum(jnp.where(remote, rank, 0), width - 1)
                row = pl.ds(pl.multiple_of((field * width + rank) * 64, 64), 64)
                if axis == 2:
                    far = got[4][row, :].astype(F32)
                    value = jnp.where(remote, far, 0.0)
                else:
                    even = (bits[axis] ^ side) == 1
                    far = jnp.where(even, got[2 * axis][row, :], got[2 * axis + 1][row, :])
                    near = face_of(x, jnp.where(valid, slot, 0), axis, 0 if side else 7)
                    value = jnp.where(valid, jnp.where(remote, far.astype(F32), near), 0.0)
                faces[axis][n, side] = value


def build(wide, odd, x, faces):
    k_of = lax.broadcasted_iota(jnp.int32, (10, 8, 128), 1)
    at_low, at_high = k_of == 0, k_of == 7
    none = jnp.zeros((1, 8, 128), F32)

    def block(n, carry):
        for i in range(10):
            if i in (0, 9):
                core = faces[0][n, 0 if i == 0 else 1].reshape(8, 8, 128)
                layers = jnp.concatenate((none, core, none), axis=0)
                low, high = jnp.zeros_like(layers), jnp.zeros_like(layers)
            else:
                at = pl.ds((i - 1) * 8, 8)
                core = x[n, pl.ds((i - 1) * 64, 64), :].reshape(8, 8, 128)
                layers = jnp.concatenate(
                    (faces[1][n, 0, at, :][None], core, faces[1][n, 1, at, :][None]), axis=0
                )
                low, high = (
                    jnp.concatenate(
                        (none, jnp.broadcast_to(faces[2][n, side, at, :][:, None, :], (8, 8, 128)), none),
                        axis=0,
                    )
                    for side in range(2)
                )
            before = jnp.where(at_low, low, pltpu.roll(layers, 1, 1))
            after = jnp.where(at_high, high, pltpu.roll(layers, 7, 1))
            for tk, shifted in enumerate((before, layers, after)):
                wide[tk, n, i] = shifted.reshape(80, 128).astype(BF)
                odd[tk, n, i] = shifted[1:9].reshape(64, 128).astype(BF)
        return carry

    lax.fori_loop(0, 4, block, 0)


def tap(wide, odd, n, i, tj, tk):
    if tj == 1:
        return odd[tk, n, i]
    return wide[tk, n, i, pl.ds(8 * tj, 64), :]


def convolve(wide, odd, pair_weights, n):
    columns = []
    for layer in range(4):
        for tj in range(3):
            for tk in range(3):
                columns.append(
                    jnp.concatenate([tap(wide, odd, n, 2 * p + layer, tj, tk) for p in range(4)], axis=0)
                )
    group = jnp.concatenate(columns, axis=1)
    both = jnp.dot(group, pair_weights[...], preferred_element_type=F32)
    rows = []
    for p in range(4):
        for half in range(2):
            rows.append(both[p * 64 : (p + 1) * 64, half * 128 : (half + 1) * 128])
    return jnp.concatenate(rows, axis=0)


def lay_weights(pair_weights, block_of):
    pair_weights[pl.ds(3456, 1152), pl.ds(0, 128)] = jnp.zeros((1152, 128), BF)
    pair_weights[pl.ds(0, 1152), pl.ds(128, 128)] = jnp.zeros((1152, 128), BF)
    for t in range(27):
        block = block_of(t)
        pair_weights[pl.ds(t * 128, 128), pl.ds(0, 128)] = block
        pair_weights[pl.ds((t + 9) * 128, 128), pl.ds(128, 128)] = block


def weight_terms(wide, odd, turned, put):
    for ti in range(3):
        columns = []
        for tj in range(3):
            for tk in range(3):
                columns.append(
                    jnp.concatenate(
                        [tap(wide, odd, n, i + ti, tj, tk) for n in range(4) for i in range(8)], axis=0
                    )
                )
        total = jnp.dot(turned[...], jnp.concatenate(columns, axis=1), preferred_element_type=F32)
        for q in range(9):
            put(9 * ti + q, total[:, q * 128 : (q + 1) * 128])


def fetch(sems, *pairs):
    copies = [pltpu.make_async_copy(a, b, sems.at[q]) for q, (a, b) in enumerate(pairs)]
    for copy in copies:
        copy.start()
    return copies


def first_faces_kernel(voxels, cotangent, links_in, occupied_in, *rest):
    sends, (masked, grad_out), (x, g, raw_x, raw_g, links, occupied, sems) = rest[:5], rest[5:7], rest[7:]
    device = lax.axis_index(SPACE)
    copies = fetch(
        sems, (links_in, links), (occupied_in, occupied), (voxels, raw_x), (cotangent, raw_g)
    )
    copies[0].wait()
    copies[1].wait()
    for copy, raw, wide, kept in ((copies[2], raw_x, x, masked), (copies[3], raw_g, g, grad_out)):
        copy.wait()
        for n in range(4):
            value = raw[0, n].astype(F32) * occupied[0, n].astype(F32)
            wide[n] = value
            kept[n] = value.astype(BF)
    pack_faces((x, g), links, device, sends)


def hidden_faces_kernel(hidden, links_in, *rest):
    sends, (x, links, sems) = rest[:5], rest[5:]
    device = lax.axis_index(SPACE)
    copies = fetch(sems, (links_in, links))
    for n in range(4):
        x[n] = hidden[n].astype(F32)
    copies[0].wait()
    pack_faces((x,), links, device, sends)


def main_kernel(
    masked, grad_out, links_in, occupied_in, first_in, second_in, g0, g1, g2, g3, g4,
    hidden, own_terms, other_terms,
    x, fx, fy, fz, wide, odd, wide_grad, odd_grad, pair_weights, slope, hidden_turned, grad_turned,
    first_weight, second_weight, links, occupied, sems,
):
    copies = fetch(
        sems,
        (links_in, links),
        (occupied_in, occupied),
        (first_in, first_weight),
        (second_in, second_weight),
    )
    device = lax.axis_index(SPACE)
    got = (g0, g1, g2, g3, g4)
    faces = (fx, fy, fz)
    for n in range(4):
        x[n] = masked[n].astype(F32)
    copies[0].wait()
    copies[1].wait()
    take_faces(x, links, device, got, 0, faces)
    build(wide, odd, x, faces)
    copies[2].wait()
    lay_weights(pair_weights, lambda t: first_weight[t])

    def forward(n, carry):
        keep = occupied[0, n].astype(F32)
        first = convolve(wide, odd, pair_weights, n)
        sigma = jax.nn.sigmoid(first)
        value = (first * sigma * keep).astype(BF)
        hidden[n] = value
        hidden_turned[:, pl.ds(pl.multiple_of(n * 512, 512), 512)] = value.T
        slope[n] = sigma * (1.0 + first * (1.0 - sigma)) * keep
        return carry

    lax.fori_loop(0, 4, forward, 0)

    for n in range(4):
        x[n] = grad_out[n].astype(F32)
    take_faces(x, links, device, got, 1, faces)
    build(wide_grad, odd_grad, x, faces)
    copies[3].wait()
    lay_weights(pair_weights, lambda t: second_weight[26 - t].T)

    core = device & 1

    def put(of_core, t, block):
        rows = pl.ds(t * 128, 128)

        @pl.when(core == of_core)
        def _():
            own_terms[rows, :] = block

        @pl.when(core != of_core)
        def _():
            other_terms[rows, :] = block

    def put_second(t, block):
        put(1, 26 - t, block)

    weight_terms(wide_grad, odd_grad, hidden_turned, put_second)

    def backward(n, carry):
        grad = convolve(wide_grad, odd_grad, pair_weights, n) * slope[n]
        grad_turned[:, pl.ds(pl.multiple_of(n * 512, 512), 512)] = grad.astype(BF).T
        return carry

    lax.fori_loop(0, 4, backward, 0)

    def put_first(t, block):
        put(0, t, block.T)

    weight_terms(wide, odd, grad_turned, put_first)


def last_kernel(
    masked, hidden, links_in, occupied_in, second_in, g0, g1, g2, g3, g4,
    output,
    x, fx, fy, fz, wide, odd, pair_weights, second_weight, links, occupied, sems,
):
    copies = fetch(
        sems, (links_in, links), (occupied_in, occupied), (second_in, second_weight)
    )
    device = lax.axis_index(SPACE)
    faces = (fx, fy, fz)
    for n in range(4):
        x[n] = hidden[n].astype(F32)
    copies[0].wait()
    copies[1].wait()
    take_faces(x, links, device, (g0, g1, g2, g3, g4), 0, faces)
    build(wide, odd, x, faces)
    copies[2].wait()
    lay_weights(pair_weights, lambda t: second_weight[t])

    def forward(n, carry):
        keep = occupied[0, n].astype(F32)
        second = convolve(wide, odd, pair_weights, n)
        output[0, n] = ((masked[n].astype(F32) + second) * keep).astype(BF)
        return carry

    lax.fori_loop(0, 4, forward, 0)


def pair_kernel(own, other, terms):
    terms[pl.ds(0, ROWS), :] = (own[...] + other[...]).astype(BF)
    terms[pl.ds(ROWS, 64 * CHUNK - ROWS), :] = jnp.zeros((64 * CHUNK - ROWS, 128), BF)


def sum_kernel(chunks, *rest):
    spread = rest[-1]
    total = chunks[0].astype(F32)

    def add(p, total):
        return total + chunks[p].astype(F32)

    total = lax.fori_loop(1, 64, add, total, unroll=7).astype(BF)

    def put(p, carry):
        spread[p] = total
        return carry

    lax.fori_loop(0, 64, put, 0, unroll=8)


def finish(core_of_first, source, outs, wide, sems):
    core = lax.axis_index("core")
    parts = 4
    rows = ROWS // parts
    for q in range(parts):
        at = pl.ds(q * rows, rows)
        wide[at, :] = source[at, :].astype(F32)
        for out, there in zip(outs, (core == core_of_first, core != core_of_first)):

            @pl.when(there)
            def _():
                pltpu.make_async_copy(wide.at[at], out.at[at], sems.at[q]).start()

    for q in range(parts):
        at = pl.ds(q * rows, rows)
        pltpu.make_async_copy(wide.at[at], outs[0].at[at], sems.at[q]).wait()


def finish_own_kernel(own, first_grad, second_grad, wide, sems):
    finish(0, own, (first_grad, second_grad), wide, sems)


def finish_other_kernel(other, first_in, second_in, first_grad, second_grad, wide, sems):
    finish(1, other, (first_grad, second_grad), wide, sems)


def send_shapes(fields):
    return tuple(jax.ShapeDtypeStruct((fields * w * 64, 128), BF) for w in (2, 2, 2, 2, 4))


def call(kernel, outs, ins, specs, scratch, limit, flops=0, nbytes=0, out_specs=VMEM, aliases={}):
    many = isinstance(outs, tuple)
    ins = [
        pltpu.with_memory_space_constraint(a, pltpu.HBM) if spec is HBM else a
        for a, spec in zip(ins, specs)
    ]
    return pl.pallas_call(
        kernel,
        out_shape=outs,
        in_specs=specs,
        out_specs=tuple(out_specs for _ in outs) if many else out_specs,
        scratch_shapes=scratch,
        input_output_aliases=aliases,
        compiler_params=pltpu.CompilerParams(vmem_limit_bytes=limit << 20),
        cost_estimate=pl.CostEstimate(flops=flops, bytes_accessed=nbytes, transcendentals=0),
    )(*ins)


def step(voxels, occupied, neighbours, first_weight, second_weight, cotangent):
    field = pltpu.VMEM((4, 512, 128), F32)
    raw = pltpu.VMEM((1, 4, 512, 128), BF)
    links = pltpu.SMEM((1, 4, 6), jnp.int32)
    flags = pltpu.SMEM((1, 4), jnp.int32)
    weights = pltpu.VMEM((27, 128, 128), BF)
    sides = [pltpu.VMEM((4, 2, 64, 128), F32)] * 3
    padded = [pltpu.VMEM((3, 4, 10, 80, 128), BF), pltpu.VMEM((3, 4, 10, 64, 128), BF)]
    pairs = pltpu.VMEM((4608, 256), BF)
    turned = pltpu.VMEM((128, 2048), BF)
    sems = pltpu.SemaphoreType.DMA((4,))
    blocks = jax.ShapeDtypeStruct((4, 512, 128), BF)
    terms_shape = jax.ShapeDtypeStruct((ROWS, 128), F32)

    *sent, masked, grad_out = call(
        first_faces_kernel,
        send_shapes(2) + (blocks, blocks),
        (voxels, cotangent, neighbours, occupied),
        [HBM] * 4,
        [field, field, raw, raw, links, flags, sems],
        10,
        nbytes=2 << 20,
    )
    got = exchange(sent)
    hidden, own, other = call(
        main_kernel,
        (blocks, terms_shape, terms_shape),
        (masked, grad_out, neighbours, occupied, first_weight, second_weight) + got,
        [VMEM] * 2 + [HBM] * 4 + [VMEM] * 5,
        [field] + sides + padded + padded + [pairs, field, turned, turned, weights, weights, links, flags, sems],
        32,
        flops=8 << 30,
        nbytes=8 << 20,
    )
    other = lax.ppermute(other, "core", PARTNER)
    chunks = jax.ShapeDtypeStruct((64 * CHUNK, 128), BF)
    terms = call(pair_kernel, chunks, (own, other), [VMEM] * 2, [], 8, nbytes=4 << 20)
    parts = lax.all_to_all(
        terms.reshape(64, CHUNK, 128), PEERS, split_axis=0, concat_axis=0, tiled=True
    )
    sent = call(
        hidden_faces_kernel,
        send_shapes(1),
        (hidden, neighbours),
        [VMEM, HBM],
        [field, links, sems],
        6,
        nbytes=1 << 20,
    )
    got = exchange(sent)
    spread = call(
        sum_kernel,
        jax.ShapeDtypeStruct((64, CHUNK, 128), BF),
        (parts,) + tuple(sent),
        [VMEM] + [ANY] * 5,
        [],
        6,
        nbytes=2 << 20,
    )
    mine = lax.all_to_all(spread, PEERS, split_axis=0, concat_axis=0, tiled=True)
    output = call(
        last_kernel,
        jax.ShapeDtypeStruct((1, 4, 512, 128), BF),
        (masked, hidden, neighbours, occupied, second_weight) + got,
        [VMEM] * 2 + [HBM] * 3 + [VMEM] * 5,
        [field] + sides + padded + [pairs, weights, links, flags, sems],
        20,
        flops=3 << 30,
        nbytes=4 << 20,
    )
    mine, output = lax.optimization_barrier((mine, output))
    mine = mine.reshape(64 * CHUNK, 128)
    theirs = lax.ppermute(mine, "core", PARTNER)
    wide = pltpu.VMEM((ROWS, 128), F32)
    grads = call(
        finish_own_kernel, (terms_shape, terms_shape), (mine,), [VMEM], [wide, sems], 4, nbytes=3 << 20, out_specs=HBM
    )
    first_grad, second_grad = call(
        finish_other_kernel,
        (terms_shape, terms_shape),
        (theirs,) + tuple(grads),
        [VMEM, HBM, HBM],
        [wide, sems],
        4,
        nbytes=3 << 20,
        out_specs=HBM,
        aliases={1: 0, 2: 1},
    )
    return output, first_grad.reshape(27, 128, 128), second_grad.reshape(27, 128, 128)


def solution(mesh):
    mesh = jax.sharding.Mesh(mesh.devices.reshape(16, 2, 4), ("chip", "core", "rep"))
    placed = (
        P("rep", SPACE, None, None),
        P("rep", SPACE),
        P("rep", SPACE, None),
        P(),
        P(),
        P("rep", SPACE, None, None),
    )
    return jax.shard_map(
        step,
        mesh=mesh,
        in_specs=placed,
        out_specs=(P("rep", SPACE, None, None), P(), P()),
        check_vma=False,
    )
```

```python
import jax
import jax.numpy as jnp
from jax import lax
from jax.experimental import pallas as pl
from jax.experimental.pallas import tpu as pltpu
from jax.sharding import PartitionSpec as P


BF = jnp.bfloat16
F32 = jnp.float32
VMEM = pl.BlockSpec(memory_space=pltpu.VMEM)
HBM = pl.BlockSpec(memory_space=pltpu.HBM)
ANY = pl.BlockSpec(memory_space=pl.ANY)
ROWS = 3456
CHUNK = 56


def tile_of(s):
    return (s & 1) | ((s >> 1) & 2), ((s >> 1) & 1) | ((s >> 2) & 2), s >> 4


def owner_of(a, b, z):
    return (a & 1) | ((b & 1) << 1) | ((a >> 1) << 2) | ((b >> 1) << 3) | (z << 4)


def swaps(kind):
    pairs = []
    for s in range(32):
        a, b, z = tile_of(s)
        if kind == "xe":
            a ^= 1
        elif kind == "ye":
            b ^= 1
        elif kind == "z":
            z ^= 1
        elif kind == "xo":
            a = 3 - a
        elif kind == "yo":
            b = 3 - b
        pairs.append((s, owner_of(a, b, z)))
    return pairs


SWAPS = tuple(swaps(kind) for kind in ("xe", "xo", "ye", "yo", "z"))


SPACE = ("z", "x", "core")
PEERS = ("x", "rep", "z")
PARTNER = ((0, 1), (1, 0))


def exchange(sent):
    got = []
    for way in range(5):
        got.append(lax.ppermute(sent[way], SPACE, SWAPS[way]))
    return tuple(got)


def remote_links(links, face, device):
    found = []
    for n in range(4):
        link = links[0, n, face]
        valid = link >= 0
        found.append((link, valid, valid & ((link >> 2) != device)))
    return found


def face_of(x, n, axis, layer):
    if axis == 0:
        return x[n, pl.ds(layer * 64, 64), :]
    if axis == 1:
        return jnp.concatenate([x[n, pl.ds(i * 64 + layer * 8, 8), :] for i in range(8)], axis=0)
    return x[n, pl.ds(layer, 64, stride=8), :]


def pack_faces(fields, links, device, sends):
    bits = (device & 1, (device >> 1) & 1, device >> 4)
    for axis in range(3):
        width = 4 if axis == 2 else 2
        for odd in range(1 if axis == 2 else 2):
            send = sends[2 * axis + odd]
            side = bits[axis] ^ (1 - odd)
            rank = jnp.int32(0)
            for n in range(4):
                link = links[0, n, 2 * axis + side]
                remote = (link >= 0) & ((link >> 2) != device)
                at = rank

                @pl.when(remote)
                def _():
                    for a, x in enumerate(fields):
                        row = pl.multiple_of((a * width + at) * 64, 64)
                        send[pl.ds(row, 64), :] = face_of(x, n, axis, side * 7).astype(BF)

                rank = rank + remote.astype(jnp.int32)


def take_faces(x, links, device, got, field, faces):
    bits = (device & 1, (device >> 1) & 1, device >> 4)
    for axis in range(3):
        width = 4 if axis == 2 else 2
        for side in range(2):
            found = remote_links(links, 2 * axis + side, device)
            for n in range(4):
                link, valid, remote = found[n]
                slot = link & 3
                rank = jnp.int32(0)
                for q in range(4):
                    if q != n:
                        lower = found[q][2] & ((found[q][0] & 3) < slot)
                        rank = rank + lower.astype(jnp.int32)
                rank = jnp.minimum(jnp.where(remote, rank, 0), width - 1)
                row = pl.ds(pl.multiple_of((field * width + rank) * 64, 64), 64)
                if axis == 2:
                    far = got[4][row, :].astype(F32)
                    value = jnp.where(remote, far, 0.0)
                else:
                    even = (bits[axis] ^ side) == 1
                    far = jnp.where(even, got[2 * axis][row, :], got[2 * axis + 1][row, :])
                    near = face_of(x, jnp.where(valid, slot, 0), axis, 0 if side else 7)
                    value = jnp.where(valid, jnp.where(remote, far.astype(F32), near), 0.0)
                faces[axis][n, side] = value


def build(wide, odd, x, faces):
    k_of = lax.broadcasted_iota(jnp.int32, (10, 8, 128), 1)
    at_low, at_high = k_of == 0, k_of == 7
    none = jnp.zeros((1, 8, 128), F32)

    def block(n, carry):
        for i in range(10):
            if i in (0, 9):
                core = faces[0][n, 0 if i == 0 else 1].reshape(8, 8, 128)
                layers = jnp.concatenate((none, core, none), axis=0)
                low, high = jnp.zeros_like(layers), jnp.zeros_like(layers)
            else:
                at = pl.ds((i - 1) * 8, 8)
                core = x[n, pl.ds((i - 1) * 64, 64), :].reshape(8, 8, 128)
                layers = jnp.concatenate(
                    (faces[1][n, 0, at, :][None], core, faces[1][n, 1, at, :][None]), axis=0
                )
                low, high = (
                    jnp.concatenate(
                        (none, jnp.broadcast_to(faces[2][n, side, at, :][:, None, :], (8, 8, 128)), none),
                        axis=0,
                    )
                    for side in range(2)
                )
            before = jnp.where(at_low, low, pltpu.roll(layers, 1, 1))
            after = jnp.where(at_high, high, pltpu.roll(layers, 7, 1))
            for tk, shifted in enumerate((before, layers, after)):
                wide[tk, n, i] = shifted.reshape(80, 128).astype(BF)
                odd[tk, n, i] = shifted[1:9].reshape(64, 128).astype(BF)
        return carry

    lax.fori_loop(0, 4, block, 0)


def tap(wide, odd, n, i, tj, tk):
    if tj == 1:
        return odd[tk, n, i]
    return wide[tk, n, i, pl.ds(8 * tj, 64), :]


def convolve(wide, odd, pair_weights, n):
    columns = []
    for layer in range(4):
        for tj in range(3):
            for tk in range(3):
                columns.append(
                    jnp.concatenate([tap(wide, odd, n, 2 * p + layer, tj, tk) for p in range(4)], axis=0)
                )
    group = jnp.concatenate(columns, axis=1)
    both = jnp.dot(group, pair_weights[...], preferred_element_type=F32)
    rows = []
    for p in range(4):
        for half in range(2):
            rows.append(both[p * 64 : (p + 1) * 64, half * 128 : (half + 1) * 128])
    return jnp.concatenate(rows, axis=0)


def lay_weights(pair_weights, block_of):
    pair_weights[pl.ds(3456, 1152), pl.ds(0, 128)] = jnp.zeros((1152, 128), BF)
    pair_weights[pl.ds(0, 1152), pl.ds(128, 128)] = jnp.zeros((1152, 128), BF)
    for t in range(27):
        block = block_of(t)
        pair_weights[pl.ds(t * 128, 128), pl.ds(0, 128)] = block
        pair_weights[pl.ds((t + 9) * 128, 128), pl.ds(128, 128)] = block


def weight_terms(wide, odd, turned, put):
    for ti in range(3):
        columns = []
        for tj in range(3):
            for tk in range(3):
                columns.append(
                    jnp.concatenate(
                        [tap(wide, odd, n, i + ti, tj, tk) for n in range(4) for i in range(8)], axis=0
                    )
                )
        total = jnp.dot(turned[...], jnp.concatenate(columns, axis=1), preferred_element_type=F32)
        for q in range(9):
            put(9 * ti + q, total[:, q * 128 : (q + 1) * 128])


def fetch(sems, *pairs):
    copies = [pltpu.make_async_copy(a, b, sems.at[q]) for q, (a, b) in enumerate(pairs)]
    for copy in copies:
        copy.start()
    return copies


def first_faces_kernel(voxels, cotangent, links_in, occupied_in, *rest):
    sends, (masked, grad_out), (x, g, raw_x, raw_g, links, occupied, sems) = rest[:5], rest[5:7], rest[7:]
    device = lax.axis_index(SPACE)
    copies = fetch(
        sems, (links_in, links), (occupied_in, occupied), (voxels, raw_x), (cotangent, raw_g)
    )
    copies[0].wait()
    copies[1].wait()
    for copy, raw, wide, kept in ((copies[2], raw_x, x, masked), (copies[3], raw_g, g, grad_out)):
        copy.wait()
        for n in range(4):
            value = raw[0, n].astype(F32) * occupied[0, n].astype(F32)
            wide[n] = value
            kept[n] = value.astype(BF)
    pack_faces((x, g), links, device, sends)


def prepare_kernel(masked, grad_out, first_in, second_in, x, g, first_pairs, second_pairs, first_weight, second_weight, sems):
    copies = fetch(sems, (first_in, first_weight), (second_in, second_weight))
    for n in range(4):
        x[n] = masked[n].astype(F32)
        g[n] = grad_out[n].astype(F32)
    copies[0].wait()
    lay_weights(first_pairs, lambda t: first_weight[t])
    copies[1].wait()
    lay_weights(second_pairs, lambda t: second_weight[26 - t].T)


def hidden_faces_kernel(hidden, links_in, *rest):
    sends, (x, links, sems) = rest[:5], rest[5:]
    device = lax.axis_index(SPACE)
    copies = fetch(sems, (links_in, links))
    for n in range(4):
        x[n] = hidden[n].astype(F32)
    copies[0].wait()
    pack_faces((x,), links, device, sends)


def main_kernel(
    x, g, first_pairs, second_pairs, links_in, occupied_in, g0, g1, g2, g3, g4,
    hidden, own_terms, other_terms,
    fx, fy, fz, wide, odd, wide_grad, odd_grad, slope, hidden_turned, grad_turned, links, occupied, sems,
):
    copies = fetch(sems, (links_in, links), (occupied_in, occupied))
    device = lax.axis_index(SPACE)
    got = (g0, g1, g2, g3, g4)
    faces = (fx, fy, fz)
    copies[0].wait()
    copies[1].wait()
    take_faces(x, links, device, got, 0, faces)
    build(wide, odd, x, faces)

    def forward(n, carry):
        keep = occupied[0, n].astype(F32)
        first = convolve(wide, odd, first_pairs, n)
        sigma = jax.nn.sigmoid(first)
        value = (first * sigma * keep).astype(BF)
        hidden[n] = value
        hidden_turned[:, pl.ds(pl.multiple_of(n * 512, 512), 512)] = value.T
        slope[n] = sigma * (1.0 + first * (1.0 - sigma)) * keep
        return carry

    lax.fori_loop(0, 4, forward, 0)

    take_faces(g, links, device, got, 1, faces)
    build(wide_grad, odd_grad, g, faces)

    core = device & 1

    def put(of_core, t, block):
        rows = pl.ds(t * 128, 128)

        @pl.when(core == of_core)
        def _():
            own_terms[rows, :] = block

        @pl.when(core != of_core)
        def _():
            other_terms[rows, :] = block

    def put_second(t, block):
        put(1, 26 - t, block)

    weight_terms(wide_grad, odd_grad, hidden_turned, put_second)

    def backward(n, carry):
        grad = convolve(wide_grad, odd_grad, second_pairs, n) * slope[n]
        grad_turned[:, pl.ds(pl.multiple_of(n * 512, 512), 512)] = grad.astype(BF).T
        return carry

    lax.fori_loop(0, 4, backward, 0)

    def put_first(t, block):
        put(0, t, block.T)

    weight_terms(wide, odd, grad_turned, put_first)


def last_kernel(
    masked, hidden, links_in, occupied_in, second_in, g0, g1, g2, g3, g4,
    output,
    x, fx, fy, fz, wide, odd, pair_weights, second_weight, links, occupied, sems,
):
    copies = fetch(
        sems, (links_in, links), (occupied_in, occupied), (second_in, second_weight)
    )
    device = lax.axis_index(SPACE)
    faces = (fx, fy, fz)
    for n in range(4):
        x[n] = hidden[n].astype(F32)
    copies[0].wait()
    copies[1].wait()
    take_faces(x, links, device, (g0, g1, g2, g3, g4), 0, faces)
    build(wide, odd, x, faces)
    copies[2].wait()
    lay_weights(pair_weights, lambda t: second_weight[t])

    def forward(n, carry):
        keep = occupied[0, n].astype(F32)
        second = convolve(wide, odd, pair_weights, n)
        output[0, n] = ((masked[n].astype(F32) + second) * keep).astype(BF)
        return carry

    lax.fori_loop(0, 4, forward, 0)


def pair_kernel(own, other, terms):
    terms[pl.ds(0, ROWS), :] = (own[...] + other[...]).astype(BF)
    terms[pl.ds(ROWS, 64 * CHUNK - ROWS), :] = jnp.zeros((64 * CHUNK - ROWS, 128), BF)


def sum_kernel(chunks, *rest):
    spread = rest[-1]
    total = chunks[0].astype(F32)

    def add(p, total):
        return total + chunks[p].astype(F32)

    total = lax.fori_loop(1, 64, add, total, unroll=7).astype(BF)

    def put(p, carry):
        spread[p] = total
        return carry

    lax.fori_loop(0, 64, put, 0, unroll=8)


def finish(core_of_first, source, outs, wide, sems):
    core = lax.axis_index("core")
    parts = 4
    rows = ROWS // parts
    for q in range(parts):
        at = pl.ds(q * rows, rows)
        wide[at, :] = source[at, :].astype(F32)
        for out, there in zip(outs, (core == core_of_first, core != core_of_first)):

            @pl.when(there)
            def _():
                pltpu.make_async_copy(wide.at[at], out.at[at], sems.at[q]).start()

    for q in range(parts):
        at = pl.ds(q * rows, rows)
        pltpu.make_async_copy(wide.at[at], outs[0].at[at], sems.at[q]).wait()


def finish_own_kernel(own, first_grad, second_grad, wide, sems):
    finish(0, own, (first_grad, second_grad), wide, sems)


def finish_other_kernel(other, first_in, second_in, first_grad, second_grad, wide, sems):
    finish(1, other, (first_grad, second_grad), wide, sems)


def send_shapes(fields):
    return tuple(jax.ShapeDtypeStruct((fields * w * 64, 128), BF) for w in (2, 2, 2, 2, 4))


def call(kernel, outs, ins, specs, scratch, limit, flops=0, nbytes=0, out_specs=VMEM, aliases={}):
    many = isinstance(outs, tuple)
    ins = [
        pltpu.with_memory_space_constraint(a, pltpu.HBM) if spec is HBM else a
        for a, spec in zip(ins, specs)
    ]
    return pl.pallas_call(
        kernel,
        out_shape=outs,
        in_specs=specs,
        out_specs=tuple(out_specs for _ in outs) if many else out_specs,
        scratch_shapes=scratch,
        input_output_aliases=aliases,
        compiler_params=pltpu.CompilerParams(vmem_limit_bytes=limit << 20),
        cost_estimate=pl.CostEstimate(flops=flops, bytes_accessed=nbytes, transcendentals=0),
    )(*ins)


def in_vmem(shape, dtype):
    return pltpu.VMEM(shape, dtype)


def step(voxels, occupied, neighbours, first_weight, second_weight, cotangent):
    field = pltpu.VMEM((4, 512, 128), F32)
    raw = pltpu.VMEM((1, 4, 512, 128), BF)
    links = pltpu.SMEM((1, 4, 6), jnp.int32)
    flags = pltpu.SMEM((1, 4), jnp.int32)
    weights = pltpu.VMEM((27, 128, 128), BF)
    sides = [pltpu.VMEM((4, 2, 64, 128), F32)] * 3
    padded = [pltpu.VMEM((3, 4, 10, 80, 128), BF), pltpu.VMEM((3, 4, 10, 64, 128), BF)]
    pairs = pltpu.VMEM((4608, 256), BF)
    turned = pltpu.VMEM((128, 2048), BF)
    sems = pltpu.SemaphoreType.DMA((4,))
    blocks = jax.ShapeDtypeStruct((4, 512, 128), BF)
    terms_shape = jax.ShapeDtypeStruct((ROWS, 128), F32)

    *sent, masked, grad_out = call(
        first_faces_kernel,
        send_shapes(2) + (blocks, blocks),
        (voxels, cotangent, neighbours, occupied),
        [HBM] * 4,
        [field, field, raw, raw, links, flags, sems],
        10,
        nbytes=2 << 20,
    )
    got = exchange(sent)
    prepared = call(
        prepare_kernel,
        (in_vmem((4, 512, 128), F32),) * 2 + (in_vmem((4608, 256), BF),) * 2,
        (masked, grad_out, first_weight, second_weight),
        [VMEM] * 2 + [HBM] * 2,
        [weights, weights, sems],
        6,
        flops=1 << 20,
        nbytes=8 << 20,
    )
    hidden, own, other = call(
        main_kernel,
        (blocks, terms_shape, terms_shape),
        tuple(prepared) + (neighbours, occupied) + got,
        [VMEM] * 4 + [HBM] * 2 + [VMEM] * 5,
        sides + padded + padded + [field, turned, turned, links, flags, sems],
        26,
        flops=8 << 30,
        nbytes=8 << 20,
    )
    other = lax.ppermute(other, "core", PARTNER)
    chunks = jax.ShapeDtypeStruct((64 * CHUNK, 128), BF)
    terms = call(pair_kernel, chunks, (own, other), [VMEM] * 2, [], 8, nbytes=4 << 20)
    parts = lax.all_to_all(
        terms.reshape(64, CHUNK, 128), PEERS, split_axis=0, concat_axis=0, tiled=True
    )
    sent = call(
        hidden_faces_kernel,
        send_shapes(1),
        (hidden, neighbours),
        [VMEM, HBM],
        [field, links, sems],
        6,
        nbytes=1 << 20,
    )
    got = exchange(sent)
    spread = call(
        sum_kernel,
        jax.ShapeDtypeStruct((64, CHUNK, 128), BF),
        (parts,) + tuple(sent),
        [VMEM] + [ANY] * 5,
        [],
        6,
        nbytes=2 << 20,
    )
    mine = lax.all_to_all(spread, PEERS, split_axis=0, concat_axis=0, tiled=True)
    output = call(
        last_kernel,
        jax.ShapeDtypeStruct((1, 4, 512, 128), BF),
        (masked, hidden, neighbours, occupied, second_weight) + got,
        [VMEM] * 2 + [HBM] * 3 + [VMEM] * 5,
        [field] + sides + padded + [pairs, weights, links, flags, sems],
        20,
        flops=3 << 30,
        nbytes=4 << 20,
    )
    mine, output = lax.optimization_barrier((mine, output))
    mine = mine.reshape(64 * CHUNK, 128)
    theirs = lax.ppermute(mine, "core", PARTNER)
    wide = pltpu.VMEM((ROWS, 128), F32)
    grads = call(
        finish_own_kernel, (terms_shape, terms_shape), (mine,), [VMEM], [wide, sems], 4, nbytes=3 << 20, out_specs=HBM
    )
    first_grad, second_grad = call(
        finish_other_kernel,
        (terms_shape, terms_shape),
        (theirs,) + tuple(grads),
        [VMEM, HBM, HBM],
        [wide, sems],
        4,
        nbytes=3 << 20,
        out_specs=HBM,
        aliases={1: 0, 2: 1},
    )
    return output, first_grad.reshape(27, 128, 128), second_grad.reshape(27, 128, 128)


def solution(mesh):
    mesh = jax.sharding.Mesh(mesh.devices.reshape(4, 4, 2, 4), ("z", "x", "core", "rep"))
    placed = (
        P("rep", SPACE, None, None),
        P("rep", SPACE),
        P("rep", SPACE, None),
        P(),
        P(),
        P("rep", SPACE, None, None),
    )
    return jax.shard_map(
        step,
        mesh=mesh,
        in_specs=placed,
        out_specs=(P("rep", SPACE, None, None), P(), P()),
        check_vma=False,
    )
```

```python
import jax
import jax.numpy as jnp
from jax import lax
from jax.experimental import pallas as pl
from jax.experimental.pallas import tpu as pltpu
from jax.sharding import PartitionSpec as P


BF = jnp.bfloat16
F32 = jnp.float32
VMEM = pl.BlockSpec(memory_space=pltpu.VMEM)
HBM = pl.BlockSpec(memory_space=pltpu.HBM)
ANY = pl.BlockSpec(memory_space=pl.ANY)
ROWS = 3456
SLOTS = 2
CHUNK = 56


def tile_of(s):
    return (s & 1) | ((s >> 1) & 2), ((s >> 1) & 1) | ((s >> 2) & 2), s >> 4


def owner_of(a, b, z):
    return (a & 1) | ((b & 1) << 1) | ((a >> 1) << 2) | ((b >> 1) << 3) | (z << 4)


def swaps(kind):
    pairs = []
    for s in range(32):
        a, b, z = tile_of(s)
        if kind == "xe":
            a ^= 1
        elif kind == "ye":
            b ^= 1
        elif kind == "z":
            z ^= 1
        elif kind == "xo":
            a = 3 - a
        elif kind == "yo":
            b = 3 - b
        pairs.append((s, owner_of(a, b, z)))
    return pairs


SWAPS = tuple(swaps(kind) for kind in ("xe", "xo", "ye", "yo", "z"))


SPACE = ("z", "x", "core")
PEERS = ("x", "rep", "z")
PARTNER = ((0, 1), (1, 0))


def exchange(sent):
    got = []
    for way in range(5):
        got.append(lax.ppermute(sent[way], SPACE, SWAPS[way]))
    return tuple(got)


def remote_links(links, face, device):
    found = []
    for n in range(4):
        link = links[0, n, face]
        valid = link >= 0
        found.append((link, valid, valid & ((link >> 2) != device)))
    return found


def face_of(x, n, axis, layer):
    if axis == 0:
        return x[n, pl.ds(layer * 64, 64), :]
    if axis == 1:
        return jnp.concatenate([x[n, pl.ds(i * 64 + layer * 8, 8), :] for i in range(8)], axis=0)
    return x[n, pl.ds(layer, 64, stride=8), :]


def pack_faces(fields, links, device, sends):
    bits = (device & 1, (device >> 1) & 1, device >> 4)
    for axis in range(3):
        width = 4 if axis == 2 else 2
        for odd in range(1 if axis == 2 else 2):
            send = sends[2 * axis + odd]
            side = bits[axis] ^ (1 - odd)
            rank = jnp.int32(0)
            for n in range(4):
                link = links[0, n, 2 * axis + side]
                remote = (link >= 0) & ((link >> 2) != device)
                at = rank

                @pl.when(remote)
                def _():
                    for a, x in enumerate(fields):
                        row = pl.multiple_of((a * width + at) * 64, 64)
                        send[pl.ds(row, 64), :] = face_of(x, n, axis, side * 7).astype(BF)

                rank = rank + remote.astype(jnp.int32)


def take_faces(x, links, device, got, field, faces):
    bits = (device & 1, (device >> 1) & 1, device >> 4)
    for axis in range(3):
        width = 4 if axis == 2 else 2
        for side in range(2):
            found = remote_links(links, 2 * axis + side, device)
            for n in range(4):
                link, valid, remote = found[n]
                slot = link & 3
                rank = jnp.int32(0)
                for q in range(4):
                    if q != n:
                        lower = found[q][2] & ((found[q][0] & 3) < slot)
                        rank = rank + lower.astype(jnp.int32)
                rank = jnp.minimum(jnp.where(remote, rank, 0), width - 1)
                row = pl.ds(pl.multiple_of((field * width + rank) * 64, 64), 64)
                if axis == 2:
                    far = got[4][row, :].astype(F32)
                    value = jnp.where(remote, far, 0.0)
                else:
                    even = (bits[axis] ^ side) == 1
                    far = jnp.where(even, got[2 * axis][row, :], got[2 * axis + 1][row, :])
                    near = face_of(x, jnp.where(valid, slot, 0), axis, 0 if side else 7)
                    value = jnp.where(valid, jnp.where(remote, far.astype(F32), near), 0.0)
                faces[axis][n, side] = value


def build(wide, odd, x, faces):
    k_of = lax.broadcasted_iota(jnp.int32, (10, 8, 128), 1)
    at_low, at_high = k_of == 0, k_of == 7
    none = jnp.zeros((1, 8, 128), F32)

    def block(n, carry):
        for i in range(10):
            if i in (0, 9):
                core = faces[0][n, 0 if i == 0 else 1].reshape(8, 8, 128)
                layers = jnp.concatenate((none, core, none), axis=0)
                low, high = jnp.zeros_like(layers), jnp.zeros_like(layers)
            else:
                at = pl.ds((i - 1) * 8, 8)
                core = x[n, pl.ds((i - 1) * 64, 64), :].reshape(8, 8, 128)
                layers = jnp.concatenate(
                    (faces[1][n, 0, at, :][None], core, faces[1][n, 1, at, :][None]), axis=0
                )
                low, high = (
                    jnp.concatenate(
                        (none, jnp.broadcast_to(faces[2][n, side, at, :][:, None, :], (8, 8, 128)), none),
                        axis=0,
                    )
                    for side in range(2)
                )
            before = jnp.where(at_low, low, pltpu.roll(layers, 1, 1))
            after = jnp.where(at_high, high, pltpu.roll(layers, 7, 1))
            for tk, shifted in enumerate((before, layers, after)):
                wide[tk, n, i] = shifted.reshape(80, 128).astype(BF)
                odd[tk, n, i] = shifted[1:9].reshape(64, 128).astype(BF)
        return carry

    lax.fori_loop(0, 4, block, 0)


def tap(wide, odd, n, i, tj, tk):
    if tj == 1:
        return odd[tk, n, i]
    return wide[tk, n, i, pl.ds(8 * tj, 64), :]


def convolve(wide, odd, pair_weights, n):
    columns = []
    for layer in range(4):
        for tj in range(3):
            for tk in range(3):
                columns.append(
                    jnp.concatenate([tap(wide, odd, SLOTS * n + q, 2 * p + layer, tj, tk) for q in range(SLOTS) for p in range(4)], axis=0)
                )
    group = jnp.concatenate(columns, axis=1)
    both = jnp.dot(group, pair_weights[...], preferred_element_type=F32)
    rows = []
    for p in range(4 * SLOTS):
        for half in range(2):
            rows.append(both[p * 64 : (p + 1) * 64, half * 128 : (half + 1) * 128])
    return jnp.concatenate(rows, axis=0)


def lay_weights(pair_weights, block_of):
    pair_weights[pl.ds(3456, 1152), pl.ds(0, 128)] = jnp.zeros((1152, 128), BF)
    pair_weights[pl.ds(0, 1152), pl.ds(128, 128)] = jnp.zeros((1152, 128), BF)
    for t in range(27):
        block = block_of(t)
        pair_weights[pl.ds(t * 128, 128), pl.ds(0, 128)] = block
        pair_weights[pl.ds((t + 9) * 128, 128), pl.ds(128, 128)] = block


def weight_terms(wide, odd, turned, put):
    for ti in range(3):
        columns = []
        for tj in range(3):
            for tk in range(3):
                columns.append(
                    jnp.concatenate(
                        [tap(wide, odd, n, i + ti, tj, tk) for n in range(4) for i in range(8)], axis=0
                    )
                )
        total = jnp.dot(turned[...], jnp.concatenate(columns, axis=1), preferred_element_type=F32)
        for q in range(9):
            put(9 * ti + q, total[:, q * 128 : (q + 1) * 128])


def fetch(sems, *pairs):
    copies = [pltpu.make_async_copy(a, b, sems.at[q]) for q, (a, b) in enumerate(pairs)]
    for copy in copies:
        copy.start()
    return copies


def first_faces_kernel(voxels, cotangent, links_in, *rest):
    sends, (x, g, raw_x, raw_g, links, sems) = rest[:5], rest[5:]
    device = lax.axis_index(SPACE)
    copies = fetch(sems, (links_in, links), (voxels, raw_x), (cotangent, raw_g))
    for copy, raw, wide in ((copies[1], raw_x, x), (copies[2], raw_g, g)):
        copy.wait()
        for n in range(4):
            wide[n] = raw[0, n].astype(F32)
    copies[0].wait()
    pack_faces((x, g), links, device, sends)


def prepare_kernel(
    voxels, cotangent, occupied_in, first_in, second_in,
    x, g, first_pairs, second_pairs,
    raw_x, raw_g, first_weight, second_weight, occupied, sems,
):
    copies = fetch(
        sems,
        (occupied_in, occupied),
        (voxels, raw_x),
        (cotangent, raw_g),
        (first_in, first_weight),
        (second_in, second_weight),
    )
    copies[0].wait()
    for copy, raw, wide in ((copies[1], raw_x, x), (copies[2], raw_g, g)):
        copy.wait()
        for n in range(4):
            wide[n] = raw[0, n].astype(F32) * occupied[0, n].astype(F32)
    copies[3].wait()
    lay_weights(first_pairs, lambda t: first_weight[t])
    copies[4].wait()
    lay_weights(second_pairs, lambda t: second_weight[26 - t].T)


def hidden_faces_kernel(hidden, links_in, *rest):
    sends, (x, links, sems) = rest[:5], rest[5:]
    device = lax.axis_index(SPACE)
    copies = fetch(sems, (links_in, links))
    for n in range(4):
        x[n] = hidden[n].astype(F32)
    copies[0].wait()
    pack_faces((x,), links, device, sends)


def main_kernel(
    x, g, first_pairs, second_pairs, links_in, occupied_in, g0, g1, g2, g3, g4,
    hidden, own_terms, other_terms,
    fx, fy, fz, wide, odd, wide_grad, odd_grad, slope, hidden_turned, grad_turned, links, occupied, sems,
):
    copies = fetch(sems, (links_in, links), (occupied_in, occupied))
    device = lax.axis_index(SPACE)
    got = (g0, g1, g2, g3, g4)
    faces = (fx, fy, fz)
    copies[0].wait()
    copies[1].wait()
    take_faces(x, links, device, got, 0, faces)
    build(wide, odd, x, faces)

    def forward(n, carry):
        firsts = convolve(wide, odd, first_pairs, n)
        for q in range(SLOTS):
            m = SLOTS * n + q
            keep = occupied[0, m].astype(F32)
            first = firsts[q * 512 : (q + 1) * 512]
            sigma = jax.nn.sigmoid(first)
            value = (first * sigma * keep).astype(BF)
            hidden[m] = value
            hidden_turned[:, pl.ds(pl.multiple_of(m * 512, 512), 512)] = value.T
            slope[m] = sigma * (1.0 + first * (1.0 - sigma)) * keep
        return carry

    lax.fori_loop(0, 4 // SLOTS, forward, 0)

    take_faces(g, links, device, got, 1, faces)
    build(wide_grad, odd_grad, g, faces)

    core = device & 1

    def put(of_core, t, block):
        rows = pl.ds(t * 128, 128)

        @pl.when(core == of_core)
        def _():
            own_terms[rows, :] = block

        @pl.when(core != of_core)
        def _():
            other_terms[rows, :] = block

    def put_second(t, block):
        put(1, 26 - t, block)

    weight_terms(wide_grad, odd_grad, hidden_turned, put_second)

    def backward(n, carry):
        grads = convolve(wide_grad, odd_grad, second_pairs, n)
        for q in range(SLOTS):
            m = SLOTS * n + q
            grad = grads[q * 512 : (q + 1) * 512] * slope[m]
            grad_turned[:, pl.ds(pl.multiple_of(m * 512, 512), 512)] = grad.astype(BF).T
        return carry

    lax.fori_loop(0, 4 // SLOTS, backward, 0)

    def put_first(t, block):
        put(0, t, block.T)

    weight_terms(wide, odd, grad_turned, put_first)


def last_kernel(
    masked, hidden, links_in, occupied_in, second_in, g0, g1, g2, g3, g4,
    output,
    x, fx, fy, fz, wide, odd, pair_weights, second_weight, links, occupied, sems,
):
    copies = fetch(
        sems, (links_in, links), (occupied_in, occupied), (second_in, second_weight)
    )
    device = lax.axis_index(SPACE)
    faces = (fx, fy, fz)
    for n in range(4):
        x[n] = hidden[n].astype(F32)
    copies[0].wait()
    copies[1].wait()
    take_faces(x, links, device, (g0, g1, g2, g3, g4), 0, faces)
    build(wide, odd, x, faces)
    copies[2].wait()
    lay_weights(pair_weights, lambda t: second_weight[t])

    def forward(n, carry):
        seconds = convolve(wide, odd, pair_weights, n)
        for q in range(SLOTS):
            m = SLOTS * n + q
            keep = occupied[0, m].astype(F32)
            output[0, m] = ((masked[m] + seconds[q * 512 : (q + 1) * 512]) * keep).astype(BF)
        return carry

    lax.fori_loop(0, 4 // SLOTS, forward, 0)


def pair_kernel(own, other, terms, staged, sems):
    copies = []
    for q in range(8):
        rows = pl.ds(q * 448, 448)
        if q == 7:
            staged[pl.ds(3136, 320), :] = (own[pl.ds(3136, 320), :] + other[pl.ds(3136, 320), :]).astype(BF)
            staged[pl.ds(ROWS, 128), :] = jnp.zeros((128, 128), BF)
        else:
            staged[rows, :] = (own[rows, :] + other[rows, :]).astype(BF)
        copies.append(pltpu.make_async_copy(staged.at[rows], terms.at[rows], sems.at[q]))
        copies[-1].start()
    for copy in copies:
        copy.wait()


def sum_kernel(chunks, *rest):
    spread, total, sems = rest[-3:]
    first = chunks[0].astype(F32)

    def add(p, so_far):
        return so_far + chunks[p].astype(F32)

    total[...] = lax.fori_loop(1, 64, add, first, unroll=7).astype(BF)

    def send(p):
        return pltpu.make_async_copy(total, spread.at[p], sems.at[p])

    for p in range(64):
        send(p).start()
    for p in range(64):
        send(p).wait()


def finish(core_of_first, source, outs, wide, sems):
    core = lax.axis_index("core")
    parts = 4
    rows = ROWS // parts
    for q in range(parts):
        at = pl.ds(q * rows, rows)
        wide[at, :] = source[at, :].astype(F32)
        for out, there in zip(outs, (core == core_of_first, core != core_of_first)):

            @pl.when(there)
            def _():
                pltpu.make_async_copy(wide.at[at], out.at[at], sems.at[q]).start()

    for q in range(parts):
        at = pl.ds(q * rows, rows)
        pltpu.make_async_copy(wide.at[at], outs[0].at[at], sems.at[q]).wait()


def finish_own_kernel(own, first_grad, second_grad, wide, sems):
    finish(0, own, (first_grad, second_grad), wide, sems)


def finish_other_kernel(other, first_in, second_in, first_grad, second_grad, wide, sems):
    finish(1, other, (first_grad, second_grad), wide, sems)


def send_shapes(fields):
    return tuple(jax.ShapeDtypeStruct((fields * w * 64, 128), BF) for w in (2, 2, 2, 2, 4))


def call(kernel, outs, ins, specs, scratch, limit, flops=0, nbytes=0, out_specs=VMEM, aliases={}):
    many = isinstance(outs, tuple)
    ins = [
        pltpu.with_memory_space_constraint(a, pltpu.HBM) if spec is HBM else a
        for a, spec in zip(ins, specs)
    ]
    return pl.pallas_call(
        kernel,
        out_shape=outs,
        in_specs=specs,
        out_specs=tuple(out_specs for _ in outs) if many else out_specs,
        scratch_shapes=scratch,
        input_output_aliases=aliases,
        compiler_params=pltpu.CompilerParams(vmem_limit_bytes=limit << 20),
        cost_estimate=pl.CostEstimate(flops=flops, bytes_accessed=nbytes, transcendentals=0),
    )(*ins)


def in_vmem(shape, dtype):
    return pltpu.VMEM(shape, dtype)


def step(voxels, occupied, neighbours, first_weight, second_weight, cotangent):
    field = pltpu.VMEM((4, 512, 128), F32)
    raw = pltpu.VMEM((1, 4, 512, 128), BF)
    links = pltpu.SMEM((1, 4, 6), jnp.int32)
    flags = pltpu.SMEM((1, 4), jnp.int32)
    weights = pltpu.VMEM((27, 128, 128), BF)
    sides = [pltpu.VMEM((4, 2, 64, 128), F32)] * 3
    padded = [pltpu.VMEM((3, 4, 10, 80, 128), BF), pltpu.VMEM((3, 4, 10, 64, 128), BF)]
    pairs = pltpu.VMEM((4608, 256), BF)
    turned = pltpu.VMEM((128, 2048), BF)
    sems = pltpu.SemaphoreType.DMA((5,))
    blocks = jax.ShapeDtypeStruct((4, 512, 128), BF)
    terms_shape = jax.ShapeDtypeStruct((ROWS, 128), F32)

    sent = call(
        first_faces_kernel,
        send_shapes(2),
        (voxels, cotangent, neighbours),
        [HBM] * 3,
        [field, field, raw, raw, links, sems],
        10,
        nbytes=2 << 20,
    )
    got = exchange(sent)
    prepared = call(
        prepare_kernel,
        (in_vmem((4, 512, 128), F32),) * 2 + (in_vmem((4608, 256), BF),) * 2,
        (voxels, cotangent, occupied, first_weight, second_weight),
        [HBM] * 5,
        [raw, raw, weights, weights, flags, sems],
        8,
        flops=1 << 20,
        nbytes=8 << 20,
    )
    hidden, own, other = call(
        main_kernel,
        (blocks, terms_shape, terms_shape),
        tuple(prepared) + (neighbours, occupied) + got,
        [VMEM] * 4 + [HBM] * 2 + [VMEM] * 5,
        sides + padded + padded + [field, turned, turned, links, flags, sems],
        26,
        flops=8 << 30,
        nbytes=8 << 20,
    )
    other = lax.ppermute(other, "core", PARTNER)
    chunks = jax.ShapeDtypeStruct((64 * CHUNK, 128), BF)
    terms = call(
        pair_kernel,
        chunks,
        (own, other),
        [VMEM] * 2,
        [pltpu.VMEM((64 * CHUNK, 128), BF), pltpu.SemaphoreType.DMA((8,))],
        4,
        nbytes=4 << 20,
        out_specs=HBM,
    )
    parts = lax.all_to_all(
        terms.reshape(64, CHUNK, 128), PEERS, split_axis=0, concat_axis=0, tiled=True
    )
    sent = call(
        hidden_faces_kernel,
        send_shapes(1),
        (hidden, neighbours),
        [VMEM, HBM],
        [field, links, sems],
        6,
        nbytes=1 << 20,
    )
    got = exchange(sent)
    spread = call(
        sum_kernel,
        jax.ShapeDtypeStruct((64, CHUNK, 128), BF),
        (parts,) + tuple(sent),
        [VMEM] + [ANY] * 5,
        [pltpu.VMEM((CHUNK, 128), BF), pltpu.SemaphoreType.DMA((64,))],
        4,
        nbytes=2 << 20,
        out_specs=HBM,
    )
    mine = lax.all_to_all(spread, PEERS, split_axis=0, concat_axis=0, tiled=True)
    output = call(
        last_kernel,
        jax.ShapeDtypeStruct((1, 4, 512, 128), BF),
        (prepared[0], hidden, neighbours, occupied, second_weight) + got,
        [VMEM] * 2 + [HBM] * 3 + [VMEM] * 5,
        [field] + sides + padded + [pairs, weights, links, flags, sems],
        20,
        flops=3 << 30,
        nbytes=4 << 20,
    )
    mine, output = lax.optimization_barrier((mine, output))
    mine = mine.reshape(64 * CHUNK, 128)
    theirs = lax.ppermute(mine, "core", PARTNER)
    wide = pltpu.VMEM((ROWS, 128), F32)
    grads = call(
        finish_own_kernel, (terms_shape, terms_shape), (mine,), [VMEM], [wide, sems], 4, nbytes=3 << 20, out_specs=HBM
    )
    first_grad, second_grad = call(
        finish_other_kernel,
        (terms_shape, terms_shape),
        (theirs,) + tuple(grads),
        [VMEM, HBM, HBM],
        [wide, sems],
        4,
        nbytes=3 << 20,
        out_specs=HBM,
        aliases={1: 0, 2: 1},
    )
    return output, first_grad.reshape(27, 128, 128), second_grad.reshape(27, 128, 128)


def solution(mesh):
    mesh = jax.sharding.Mesh(mesh.devices.reshape(4, 4, 2, 4), ("z", "x", "core", "rep"))
    placed = (
        P("rep", SPACE, None, None),
        P("rep", SPACE),
        P("rep", SPACE, None),
        P(),
        P(),
        P("rep", SPACE, None, None),
    )
    return jax.shard_map(
        step,
        mesh=mesh,
        in_specs=placed,
        out_specs=(P("rep", SPACE, None, None), P(), P()),
        check_vma=False,
    )
```

```python
import jax
import jax.numpy as jnp
from jax import lax
from jax.experimental import pallas as pl
from jax.experimental.pallas import tpu as pltpu
from jax.sharding import PartitionSpec as P


BF = jnp.bfloat16
F32 = jnp.float32
VMEM = pl.BlockSpec(memory_space=pltpu.VMEM)
HBM = pl.BlockSpec(memory_space=pltpu.HBM)
ANY = pl.BlockSpec(memory_space=pl.ANY)
ROWS = 3456
SLOTS = 2
CHUNK = 56


def tile_of(s):
    return (s & 1) | ((s >> 1) & 2), ((s >> 1) & 1) | ((s >> 2) & 2), s >> 4


def owner_of(a, b, z):
    return (a & 1) | ((b & 1) << 1) | ((a >> 1) << 2) | ((b >> 1) << 3) | (z << 4)


def swaps(kind):
    pairs = []
    for s in range(32):
        a, b, z = tile_of(s)
        if kind == "xe":
            a ^= 1
        elif kind == "ye":
            b ^= 1
        elif kind == "z":
            z ^= 1
        elif kind == "xo":
            a = 3 - a
        elif kind == "yo":
            b = 3 - b
        pairs.append((s, owner_of(a, b, z)))
    return pairs


SWAPS = tuple(swaps(kind) for kind in ("xe", "xo", "ye", "yo", "z"))


SPACE = ("z", "x", "core")
PEERS = ("x", "rep", "z")
PARTNER = ((0, 1), (1, 0))


def exchange(sent):
    got = []
    for way in range(5):
        got.append(lax.ppermute(sent[way], SPACE, SWAPS[way]))
    return tuple(got)


def remote_links(links, face, device):
    found = []
    for n in range(4):
        link = links[0, n, face]
        valid = link >= 0
        found.append((link, valid, valid & ((link >> 2) != device)))
    return found


def face_of(x, n, axis, layer):
    if axis == 0:
        return x[n, pl.ds(layer * 64, 64), :]
    if axis == 1:
        return jnp.concatenate([x[n, pl.ds(i * 64 + layer * 8, 8), :] for i in range(8)], axis=0)
    return x[n, pl.ds(layer, 64, stride=8), :]


def pack_faces(fields, links, device, sends):
    bits = (device & 1, (device >> 1) & 1, device >> 4)
    for axis in range(3):
        width = 4 if axis == 2 else 2
        for odd in range(1 if axis == 2 else 2):
            send = sends[2 * axis + odd]
            side = bits[axis] ^ (1 - odd)
            rank = jnp.int32(0)
            for n in range(4):
                link = links[0, n, 2 * axis + side]
                remote = (link >= 0) & ((link >> 2) != device)
                at = rank

                @pl.when(remote)
                def _():
                    for a, x in enumerate(fields):
                        row = pl.multiple_of((a * width + at) * 64, 64)
                        send[pl.ds(row, 64), :] = face_of(x, n, axis, side * 7).astype(BF)

                rank = rank + remote.astype(jnp.int32)


def take_faces(x, links, device, got, field, faces):
    bits = (device & 1, (device >> 1) & 1, device >> 4)
    for axis in range(3):
        width = 4 if axis == 2 else 2
        for side in range(2):
            found = remote_links(links, 2 * axis + side, device)
            for n in range(4):
                link, valid, remote = found[n]
                slot = link & 3
                rank = jnp.int32(0)
                for q in range(4):
                    if q != n:
                        lower = found[q][2] & ((found[q][0] & 3) < slot)
                        rank = rank + lower.astype(jnp.int32)
                rank = jnp.minimum(jnp.where(remote, rank, 0), width - 1)
                row = pl.ds(pl.multiple_of((field * width + rank) * 64, 64), 64)
                if axis == 2:
                    far = got[4][row, :].astype(F32)
                    value = jnp.where(remote, far, 0.0)
                else:
                    even = (bits[axis] ^ side) == 1
                    far = jnp.where(even, got[2 * axis][row, :], got[2 * axis + 1][row, :])
                    near = face_of(x, jnp.where(valid, slot, 0), axis, 0 if side else 7)
                    value = jnp.where(valid, jnp.where(remote, far.astype(F32), near), 0.0)
                faces[axis][n, side] = value


def build(wide, odd, x, faces, slots):
    k_of = lax.broadcasted_iota(jnp.int32, (10, 8, 128), 1)
    at_low, at_high = k_of == 0, k_of == 7
    none = jnp.zeros((1, 8, 128), F32)

    def block(n):
        for i in range(10):
            if i in (0, 9):
                core = faces[0][n, 0 if i == 0 else 1].reshape(8, 8, 128)
                layers = jnp.concatenate((none, core, none), axis=0)
                low, high = jnp.zeros_like(layers), jnp.zeros_like(layers)
            else:
                at = pl.ds((i - 1) * 8, 8)
                core = x[n, pl.ds((i - 1) * 64, 64), :].reshape(8, 8, 128)
                layers = jnp.concatenate(
                    (faces[1][n, 0, at, :][None], core, faces[1][n, 1, at, :][None]), axis=0
                )
                low, high = (
                    jnp.concatenate(
                        (none, jnp.broadcast_to(faces[2][n, side, at, :][:, None, :], (8, 8, 128)), none),
                        axis=0,
                    )
                    for side in range(2)
                )
            before = jnp.where(at_low, low, pltpu.roll(layers, 1, 1))
            after = jnp.where(at_high, high, pltpu.roll(layers, 7, 1))
            for tk, shifted in enumerate((before, layers, after)):
                wide[tk, n, i] = shifted.reshape(80, 128).astype(BF)
                odd[tk, n, i] = shifted[1:9].reshape(64, 128).astype(BF)

    for n in slots:
        block(n)


def tap(wide, odd, n, i, tj, tk):
    if tj == 1:
        return odd[tk, n, i]
    return wide[tk, n, i, pl.ds(8 * tj, 64), :]


def convolve(wide, odd, pair_weights, n):
    columns = []
    for layer in range(4):
        for tj in range(3):
            for tk in range(3):
                columns.append(
                    jnp.concatenate([tap(wide, odd, SLOTS * n + q, 2 * p + layer, tj, tk) for q in range(SLOTS) for p in range(4)], axis=0)
                )
    group = jnp.concatenate(columns, axis=1)
    both = jnp.dot(group, pair_weights[...], preferred_element_type=F32)
    rows = []
    for p in range(4 * SLOTS):
        for half in range(2):
            rows.append(both[p * 64 : (p + 1) * 64, half * 128 : (half + 1) * 128])
    return jnp.concatenate(rows, axis=0)


def lay_weights(pair_weights, block_of):
    pair_weights[pl.ds(3456, 1152), pl.ds(0, 128)] = jnp.zeros((1152, 128), BF)
    pair_weights[pl.ds(0, 1152), pl.ds(128, 128)] = jnp.zeros((1152, 128), BF)
    for t in range(27):
        block = block_of(t)
        pair_weights[pl.ds(t * 128, 128), pl.ds(0, 128)] = block
        pair_weights[pl.ds((t + 9) * 128, 128), pl.ds(128, 128)] = block


def weight_terms(wide, odd, turned, put):
    for ti in range(3):
        columns = []
        for tj in range(3):
            for tk in range(3):
                columns.append(
                    jnp.concatenate(
                        [tap(wide, odd, n, i + ti, tj, tk) for n in range(4) for i in range(8)], axis=0
                    )
                )
        total = jnp.dot(turned[...], jnp.concatenate(columns, axis=1), preferred_element_type=F32)
        put(ti, [total[:, q * 128 : (q + 1) * 128] for q in range(9)])


def fetch(sems, *pairs):
    copies = [pltpu.make_async_copy(a, b, sems.at[q]) for q, (a, b) in enumerate(pairs)]
    for copy in copies:
        copy.start()
    return copies


def first_faces_kernel(voxels, cotangent, links_in, *rest):
    sends, (x, g, raw_x, raw_g, links, sems) = rest[:5], rest[5:]
    device = lax.axis_index(SPACE)
    copies = fetch(sems, (links_in, links), (voxels, raw_x), (cotangent, raw_g))
    for copy, raw, wide in ((copies[1], raw_x, x), (copies[2], raw_g, g)):
        copy.wait()
        for n in range(4):
            wide[n] = raw[0, n].astype(F32)
    copies[0].wait()
    pack_faces((x, g), links, device, sends)


def prepare_kernel(
    voxels, cotangent, occupied_in, first_in, second_in,
    x, g, first_pairs, second_pairs,
    raw_x, raw_g, first_weight, second_weight, occupied, sems,
):
    copies = fetch(
        sems,
        (occupied_in, occupied),
        (voxels, raw_x),
        (cotangent, raw_g),
        (first_in, first_weight),
        (second_in, second_weight),
    )
    copies[0].wait()
    for copy, raw, wide in ((copies[1], raw_x, x), (copies[2], raw_g, g)):
        copy.wait()
        for n in range(4):
            wide[n] = raw[0, n].astype(F32) * occupied[0, n].astype(F32)
    copies[3].wait()
    lay_weights(first_pairs, lambda t: first_weight[t])
    copies[4].wait()
    lay_weights(second_pairs, lambda t: second_weight[26 - t].T)


def hidden_faces_kernel(hidden, links_in, *rest):
    sends, (x, links, sems) = rest[:5], rest[5:]
    device = lax.axis_index(SPACE)
    copies = fetch(sems, (links_in, links))
    for n in range(4):
        x[n] = hidden[n].astype(F32)
    copies[0].wait()
    pack_faces((x,), links, device, sends)


def main_kernel(
    x, g, first_pairs, second_pairs, links_in, occupied_in, g0, g1, g2, g3, g4,
    hidden, own_terms, other_terms,
    fx, fy, fz, gx, gy, gz, wide, odd, wide_grad, odd_grad, slope, hidden_turned, grad_turned, links, occupied, sems,
):
    copies = fetch(sems, (links_in, links), (occupied_in, occupied))
    device = lax.axis_index(SPACE)
    got = (g0, g1, g2, g3, g4)
    faces = (fx, fy, fz)
    copies[0].wait()
    copies[1].wait()
    take_faces(x, links, device, got, 0, faces)
    take_faces(g, links, device, got, 1, (gx, gy, gz))

    def forward(n, carry):
        slots = [SLOTS * n + q for q in range(SLOTS)]
        build(wide, odd, x, faces, slots)
        build(wide_grad, odd_grad, g, (gx, gy, gz), slots)
        firsts = convolve(wide, odd, first_pairs, n)
        for q in range(SLOTS):
            m = SLOTS * n + q
            keep = occupied[0, m].astype(F32)
            first = firsts[q * 512 : (q + 1) * 512]
            sigma = jax.nn.sigmoid(first)
            value = (first * sigma * keep).astype(BF)
            hidden[m] = value
            hidden_turned[:, pl.ds(pl.multiple_of(m * 512, 512), 512)] = value.T
            slope[m] = sigma * (1.0 + first * (1.0 - sigma)) * keep
        return carry

    lax.fori_loop(0, 4 // SLOTS, forward, 0, unroll=True)


    core = device & 1

    def put(of_core, start, blocks):
        rows = pl.ds(start * 128, 1152)
        stacked = jnp.concatenate(blocks, axis=0)

        @pl.when(core == of_core)
        def _():
            own_terms[rows, :] = stacked

        @pl.when(core != of_core)
        def _():
            other_terms[rows, :] = stacked

    def put_second(ti, blocks):
        put(1, 18 - 9 * ti, blocks[::-1])

    weight_terms(wide_grad, odd_grad, hidden_turned, put_second)

    def backward(n, carry):
        grads = convolve(wide_grad, odd_grad, second_pairs, n)
        for q in range(SLOTS):
            m = SLOTS * n + q
            grad = grads[q * 512 : (q + 1) * 512] * slope[m]
            grad_turned[:, pl.ds(pl.multiple_of(m * 512, 512), 512)] = grad.astype(BF).T
        return carry

    lax.fori_loop(0, 4 // SLOTS, backward, 0, unroll=True)

    def put_first(ti, blocks):
        put(0, 9 * ti, [block.T for block in blocks])

    weight_terms(wide, odd, grad_turned, put_first)


def last_kernel(
    masked, hidden, links_in, occupied_in, second_in, g0, g1, g2, g3, g4,
    output,
    x, fx, fy, fz, wide, odd, pair_weights, second_weight, links, occupied, sems,
):
    copies = fetch(
        sems, (links_in, links), (occupied_in, occupied), (second_in, second_weight)
    )
    device = lax.axis_index(SPACE)
    faces = (fx, fy, fz)
    for n in range(4):
        x[n] = hidden[n].astype(F32)
    copies[0].wait()
    copies[1].wait()
    take_faces(x, links, device, (g0, g1, g2, g3, g4), 0, faces)
    copies[2].wait()
    lay_weights(pair_weights, lambda t: second_weight[t])

    def forward(n, carry):
        build(wide, odd, x, faces, [SLOTS * n + q for q in range(SLOTS)])
        seconds = convolve(wide, odd, pair_weights, n)
        for q in range(SLOTS):
            m = SLOTS * n + q
            keep = occupied[0, m].astype(F32)
            output[0, m] = ((masked[m] + seconds[q * 512 : (q + 1) * 512]) * keep).astype(BF)
        return carry

    lax.fori_loop(0, 4 // SLOTS, forward, 0, unroll=True)


def pair_kernel(own, other, terms, staged, sems):
    copies = []
    for q in range(8):
        rows = pl.ds(q * 448, 448)
        if q == 7:
            staged[pl.ds(3136, 320), :] = (own[pl.ds(3136, 320), :] + other[pl.ds(3136, 320), :]).astype(BF)
            staged[pl.ds(ROWS, 128), :] = jnp.zeros((128, 128), BF)
        else:
            staged[rows, :] = (own[rows, :] + other[rows, :]).astype(BF)
        copies.append(pltpu.make_async_copy(staged.at[rows], terms.at[rows], sems.at[q]))
        copies[-1].start()
    for copy in copies:
        copy.wait()


def sum_kernel(chunks, *rest):
    spread = rest[-1]
    total = chunks[0].astype(F32)

    def add(p, total):
        return total + chunks[p].astype(F32)

    total = lax.fori_loop(1, 64, add, total, unroll=7).astype(BF)

    def put(p, carry):
        spread[p] = total
        return carry

    lax.fori_loop(0, 64, put, 0, unroll=8)


def finish(core_of_first, source, outs, wide, sems):
    core = lax.axis_index("core")
    parts = 4
    rows = ROWS // parts
    for q in range(parts):
        at = pl.ds(q * rows, rows)
        wide[at, :] = source[at, :].astype(F32)
        for out, there in zip(outs, (core == core_of_first, core != core_of_first)):

            @pl.when(there)
            def _():
                pltpu.make_async_copy(wide.at[at], out.at[at], sems.at[q]).start()

    for q in range(parts):
        at = pl.ds(q * rows, rows)
        pltpu.make_async_copy(wide.at[at], outs[0].at[at], sems.at[q]).wait()


def finish_own_kernel(own, first_grad, second_grad, wide, sems):
    finish(0, own, (first_grad, second_grad), wide, sems)


def finish_other_kernel(other, first_in, second_in, first_grad, second_grad, wide, sems):
    finish(1, other, (first_grad, second_grad), wide, sems)


def send_shapes(fields):
    return tuple(jax.ShapeDtypeStruct((fields * w * 64, 128), BF) for w in (2, 2, 2, 2, 4))


def call(kernel, outs, ins, specs, scratch, limit, flops=0, nbytes=0, out_specs=VMEM, aliases={}):
    many = isinstance(outs, tuple)
    ins = [
        pltpu.with_memory_space_constraint(a, pltpu.HBM) if spec is HBM else a
        for a, spec in zip(ins, specs)
    ]
    return pl.pallas_call(
        kernel,
        out_shape=outs,
        in_specs=specs,
        out_specs=tuple(out_specs for _ in outs) if many else out_specs,
        scratch_shapes=scratch,
        input_output_aliases=aliases,
        compiler_params=pltpu.CompilerParams(vmem_limit_bytes=limit << 20),
        cost_estimate=pl.CostEstimate(flops=flops, bytes_accessed=nbytes, transcendentals=0),
    )(*ins)


def in_vmem(shape, dtype):
    return pltpu.VMEM(shape, dtype)


def step(voxels, occupied, neighbours, first_weight, second_weight, cotangent):
    field = pltpu.VMEM((4, 512, 128), F32)
    raw = pltpu.VMEM((1, 4, 512, 128), BF)
    links = pltpu.SMEM((1, 4, 6), jnp.int32)
    flags = pltpu.SMEM((1, 4), jnp.int32)
    weights = pltpu.VMEM((27, 128, 128), BF)
    sides = [pltpu.VMEM((4, 2, 64, 128), F32)] * 3
    padded = [pltpu.VMEM((3, 4, 10, 80, 128), BF), pltpu.VMEM((3, 4, 10, 64, 128), BF)]
    pairs = pltpu.VMEM((4608, 256), BF)
    turned = pltpu.VMEM((128, 2048), BF)
    sems = pltpu.SemaphoreType.DMA((5,))
    blocks = jax.ShapeDtypeStruct((4, 512, 128), BF)
    terms_shape = jax.ShapeDtypeStruct((ROWS, 128), F32)

    sent = call(
        first_faces_kernel,
        send_shapes(2),
        (voxels, cotangent, neighbours),
        [HBM] * 3,
        [field, field, raw, raw, links, sems],
        10,
        nbytes=2 << 20,
    )
    got = exchange(sent)
    prepared = call(
        prepare_kernel,
        (in_vmem((4, 512, 128), F32),) * 2 + (in_vmem((4608, 256), BF),) * 2,
        (voxels, cotangent, occupied, first_weight, second_weight),
        [HBM] * 5,
        [raw, raw, weights, weights, flags, sems],
        8,
        flops=1 << 20,
        nbytes=8 << 20,
    )
    hidden, own, other = call(
        main_kernel,
        (blocks, terms_shape, terms_shape),
        tuple(prepared) + (neighbours, occupied) + got,
        [VMEM] * 4 + [HBM] * 2 + [VMEM] * 5,
        sides + sides + padded + padded + [field, turned, turned, links, flags, sems],
        26,
        flops=8 << 30,
        nbytes=8 << 20,
    )
    other = lax.ppermute(other, "core", PARTNER)
    chunks = jax.ShapeDtypeStruct((64 * CHUNK, 128), BF)
    terms = call(
        pair_kernel,
        chunks,
        (own, other),
        [VMEM] * 2,
        [pltpu.VMEM((64 * CHUNK, 128), BF), pltpu.SemaphoreType.DMA((8,))],
        4,
        nbytes=4 << 20,
        out_specs=HBM,
    )
    parts = lax.all_to_all(
        terms.reshape(64, CHUNK, 128), PEERS, split_axis=0, concat_axis=0, tiled=True
    )
    sent = call(
        hidden_faces_kernel,
        send_shapes(1),
        (hidden, neighbours),
        [VMEM, HBM],
        [field, links, sems],
        6,
        nbytes=1 << 20,
    )
    got = exchange(sent)
    spread = call(
        sum_kernel,
        jax.ShapeDtypeStruct((64, CHUNK, 128), BF),
        (parts,) + tuple(sent),
        [VMEM] + [ANY] * 5,
        [],
        6,
        nbytes=2 << 20,
    )
    mine = lax.all_to_all(spread, PEERS, split_axis=0, concat_axis=0, tiled=True)
    output = call(
        last_kernel,
        jax.ShapeDtypeStruct((1, 4, 512, 128), BF),
        (prepared[0], hidden, neighbours, occupied, second_weight) + got,
        [VMEM] * 2 + [HBM] * 3 + [VMEM] * 5,
        [field] + sides + padded + [pairs, weights, links, flags, sems],
        20,
        flops=3 << 30,
        nbytes=4 << 20,
    )
    mine, output = lax.optimization_barrier((mine, output))
    mine = mine.reshape(64 * CHUNK, 128)
    theirs = lax.ppermute(mine, "core", PARTNER)
    wide = pltpu.VMEM((ROWS, 128), F32)
    grads = call(
        finish_own_kernel, (terms_shape, terms_shape), (mine,), [VMEM], [wide, sems], 4, nbytes=3 << 20, out_specs=HBM
    )
    first_grad, second_grad = call(
        finish_other_kernel,
        (terms_shape, terms_shape),
        (theirs,) + tuple(grads),
        [VMEM, HBM, HBM],
        [wide, sems],
        4,
        nbytes=3 << 20,
        out_specs=HBM,
        aliases={1: 0, 2: 1},
    )
    return output, first_grad.reshape(27, 128, 128), second_grad.reshape(27, 128, 128)


def solution(mesh):
    mesh = jax.sharding.Mesh(mesh.devices.reshape(4, 4, 2, 4), ("z", "x", "core", "rep"))
    placed = (
        P("rep", SPACE, None, None),
        P("rep", SPACE),
        P("rep", SPACE, None),
        P(),
        P(),
        P("rep", SPACE, None, None),
    )
    return jax.shard_map(
        step,
        mesh=mesh,
        in_specs=placed,
        out_specs=(P("rep", SPACE, None, None), P(), P()),
        check_vma=False,
    )
```

```python
import jax
import jax.numpy as jnp
from jax import lax
from jax.experimental import pallas as pl
from jax.experimental.pallas import tpu as pltpu
from jax.sharding import PartitionSpec as P


BF = jnp.bfloat16
F32 = jnp.float32
VMEM = pl.BlockSpec(memory_space=pltpu.VMEM)
HBM = pl.BlockSpec(memory_space=pltpu.HBM)
ANY = pl.BlockSpec(memory_space=pl.ANY)
ROWS = 3456
SLOTS = 2
CHUNK = 56


def tile_of(s):
    return (s & 1) | ((s >> 1) & 2), ((s >> 1) & 1) | ((s >> 2) & 2), s >> 4


def owner_of(a, b, z):
    return (a & 1) | ((b & 1) << 1) | ((a >> 1) << 2) | ((b >> 1) << 3) | (z << 4)


def swaps(kind):
    pairs = []
    for s in range(32):
        a, b, z = tile_of(s)
        if kind == "xe":
            a ^= 1
        elif kind == "ye":
            b ^= 1
        elif kind == "z":
            z ^= 1
        elif kind == "xo":
            a = 3 - a
        elif kind == "yo":
            b = 3 - b
        pairs.append((s, owner_of(a, b, z)))
    return pairs


SWAPS = tuple(swaps(kind) for kind in ("xe", "xo", "ye", "yo", "z"))


SPACE = ("z", "x", "core")
PEERS = ("x", "rep", "z")
PARTNER = ((0, 1), (1, 0))


def exchange(sent):
    got = []
    for way in range(5):
        got.append(lax.ppermute(sent[way], SPACE, SWAPS[way]))
    return tuple(got)


def remote_links(links, face, device):
    found = []
    for n in range(4):
        link = links[0, n, face]
        valid = link >= 0
        found.append((link, valid, valid & ((link >> 2) != device)))
    return found


def face_of(x, n, axis, layer):
    if axis == 0:
        return x[n, pl.ds(layer * 64, 64), :]
    if axis == 1:
        return jnp.concatenate([x[n, pl.ds(i * 64 + layer * 8, 8), :] for i in range(8)], axis=0)
    return x[n, pl.ds(layer, 64, stride=8), :]


def pack_faces(fields, links, device, sends):
    bits = (device & 1, (device >> 1) & 1, device >> 4)
    for axis in range(3):
        width = 4 if axis == 2 else 2
        for odd in range(1 if axis == 2 else 2):
            send = sends[2 * axis + odd]
            side = bits[axis] ^ (1 - odd)
            rank = jnp.int32(0)
            for n in range(4):
                link = links[0, n, 2 * axis + side]
                remote = (link >= 0) & ((link >> 2) != device)
                at = rank

                @pl.when(remote)
                def _():
                    for a, x in enumerate(fields):
                        row = pl.multiple_of((a * width + at) * 64, 64)
                        send[pl.ds(row, 64), :] = face_of(x, n, axis, side * 7).astype(BF)

                rank = rank + remote.astype(jnp.int32)


def take_faces(x, links, device, got, field, faces):
    bits = (device & 1, (device >> 1) & 1, device >> 4)
    for axis in range(3):
        width = 4 if axis == 2 else 2
        for side in range(2):
            found = remote_links(links, 2 * axis + side, device)
            for n in range(4):
                link, valid, remote = found[n]
                slot = link & 3
                rank = jnp.int32(0)
                for q in range(4):
                    if q != n:
                        lower = found[q][2] & ((found[q][0] & 3) < slot)
                        rank = rank + lower.astype(jnp.int32)
                rank = jnp.minimum(jnp.where(remote, rank, 0), width - 1)
                row = pl.ds(pl.multiple_of((field * width + rank) * 64, 64), 64)
                if axis == 2:
                    far = got[4][row, :].astype(F32)
                    value = jnp.where(remote, far, 0.0)
                else:
                    even = (bits[axis] ^ side) == 1
                    far = jnp.where(even, got[2 * axis][row, :], got[2 * axis + 1][row, :])
                    near = face_of(x, jnp.where(valid, slot, 0), axis, 0 if side else 7)
                    value = jnp.where(valid, jnp.where(remote, far.astype(F32), near), 0.0)
                faces[axis][n, side] = value


def build(wide, odd, x, faces, slots):
    k_of = lax.broadcasted_iota(jnp.int32, (10, 8, 128), 1)
    at_low, at_high = k_of == 0, k_of == 7
    none = jnp.zeros((1, 8, 128), F32)

    def block(n):
        for i in range(10):
            if i in (0, 9):
                core = faces[0][n, 0 if i == 0 else 1].reshape(8, 8, 128)
                layers = jnp.concatenate((none, core, none), axis=0)
                low, high = jnp.zeros_like(layers), jnp.zeros_like(layers)
            else:
                at = pl.ds((i - 1) * 8, 8)
                core = x[n, pl.ds((i - 1) * 64, 64), :].reshape(8, 8, 128)
                layers = jnp.concatenate(
                    (faces[1][n, 0, at, :][None], core, faces[1][n, 1, at, :][None]), axis=0
                )
                low, high = (
                    jnp.concatenate(
                        (none, jnp.broadcast_to(faces[2][n, side, at, :][:, None, :], (8, 8, 128)), none),
                        axis=0,
                    )
                    for side in range(2)
                )
            before = jnp.where(at_low, low, pltpu.roll(layers, 1, 1))
            after = jnp.where(at_high, high, pltpu.roll(layers, 7, 1))
            for tk, shifted in enumerate((before, layers, after)):
                wide[tk, n, i] = shifted.reshape(80, 128).astype(BF)
                odd[tk, n, i] = shifted[1:9].reshape(64, 128).astype(BF)

    for n in slots:
        block(n)


def tap(wide, odd, n, i, tj, tk):
    if tj == 1:
        return odd[tk, n, i]
    return wide[tk, n, i, pl.ds(8 * tj, 64), :]


def convolve(wide, odd, pair_weights, n):
    columns = []
    for layer in range(4):
        for tj in range(3):
            for tk in range(3):
                columns.append(
                    jnp.concatenate([tap(wide, odd, SLOTS * n + q, 2 * p + layer, tj, tk) for q in range(SLOTS) for p in range(4)], axis=0)
                )
    group = jnp.concatenate(columns, axis=1)
    both = jnp.dot(group, pair_weights[...], preferred_element_type=F32)
    rows = []
    for p in range(4 * SLOTS):
        for half in range(2):
            rows.append(both[p * 64 : (p + 1) * 64, half * 128 : (half + 1) * 128])
    return jnp.concatenate(rows, axis=0)


def lay_weights(pair_weights, block_of):
    pair_weights[pl.ds(3456, 1152), pl.ds(0, 128)] = jnp.zeros((1152, 128), BF)
    pair_weights[pl.ds(0, 1152), pl.ds(128, 128)] = jnp.zeros((1152, 128), BF)
    for t in range(27):
        block = block_of(t)
        pair_weights[pl.ds(t * 128, 128), pl.ds(0, 128)] = block
        pair_weights[pl.ds((t + 9) * 128, 128), pl.ds(128, 128)] = block


def weight_terms(wide, odd, turned, put):
    for ti in range(3):
        columns = []
        for tj in range(3):
            for tk in range(3):
                columns.append(
                    jnp.concatenate(
                        [tap(wide, odd, n, i + ti, tj, tk) for n in range(4) for i in range(8)], axis=0
                    )
                )
        total = jnp.dot(turned[...], jnp.concatenate(columns, axis=1), preferred_element_type=F32)
        put(ti, [total[:, q * 128 : (q + 1) * 128] for q in range(9)])


def fetch(sems, *pairs):
    copies = [pltpu.make_async_copy(a, b, sems.at[q]) for q, (a, b) in enumerate(pairs)]
    for copy in copies:
        copy.start()
    return copies


def first_faces_kernel(voxels, cotangent, links_in, *rest):
    sends, (x, g, raw_x, raw_g, links, sems) = rest[:5], rest[5:]
    device = lax.axis_index(SPACE)
    copies = fetch(sems, (links_in, links), (voxels, raw_x), (cotangent, raw_g))
    for copy, raw, wide in ((copies[1], raw_x, x), (copies[2], raw_g, g)):
        copy.wait()
        for n in range(4):
            wide[n] = raw[0, n].astype(F32)
    copies[0].wait()
    pack_faces((x, g), links, device, sends)


def prepare_kernel(
    voxels, cotangent, occupied_in, first_in, second_in,
    x, g, first_pairs, second_pairs,
    raw_x, raw_g, first_weight, second_weight, occupied, sems,
):
    copies = fetch(
        sems,
        (occupied_in, occupied),
        (voxels, raw_x),
        (cotangent, raw_g),
        (first_in, first_weight),
        (second_in, second_weight),
    )
    copies[0].wait()
    for copy, raw, wide in ((copies[1], raw_x, x), (copies[2], raw_g, g)):
        copy.wait()
        for n in range(4):
            wide[n] = raw[0, n].astype(F32) * occupied[0, n].astype(F32)
    copies[3].wait()
    lay_weights(first_pairs, lambda t: first_weight[t])
    copies[4].wait()
    lay_weights(second_pairs, lambda t: second_weight[26 - t].T)


def hidden_faces_kernel(hidden, links_in, *rest):
    sends, (x, links, sems) = rest[:5], rest[5:]
    device = lax.axis_index(SPACE)
    copies = fetch(sems, (links_in, links))
    for n in range(4):
        x[n] = hidden[n].astype(F32)
    copies[0].wait()
    pack_faces((x,), links, device, sends)


def main_kernel(
    x, g, first_pairs, second_pairs, links_in, occupied_in, g0, g1, g2, g3, g4,
    hidden, own_terms, other_terms,
    fx, fy, fz, gx, gy, gz, wide, odd, wide_grad, odd_grad, slope, hidden_turned, grad_turned, links, occupied, sems,
):
    copies = fetch(sems, (links_in, links), (occupied_in, occupied))
    device = lax.axis_index(SPACE)
    got = (g0, g1, g2, g3, g4)
    faces = (fx, fy, fz)
    copies[0].wait()
    copies[1].wait()
    take_faces(x, links, device, got, 0, faces)
    take_faces(g, links, device, got, 1, (gx, gy, gz))

    def forward(n, carry):
        slots = [SLOTS * n + q for q in range(SLOTS)]
        build(wide, odd, x, faces, slots)
        build(wide_grad, odd_grad, g, (gx, gy, gz), slots)
        firsts = convolve(wide, odd, first_pairs, n)
        for q in range(SLOTS):
            m = SLOTS * n + q
            keep = occupied[0, m].astype(F32)
            first = firsts[q * 512 : (q + 1) * 512]
            sigma = jax.nn.sigmoid(first)
            value = (first * sigma * keep).astype(BF)
            hidden[m] = value
            hidden_turned[:, pl.ds(pl.multiple_of(m * 512, 512), 512)] = value.T
            slope[m] = sigma * (1.0 + first * (1.0 - sigma)) * keep
        return carry

    lax.fori_loop(0, 4 // SLOTS, forward, 0, unroll=True)


    core = device & 1

    def put(of_core, start, blocks):
        rows = pl.ds(start * 128, 1152)
        stacked = jnp.concatenate(blocks, axis=0)

        @pl.when(core == of_core)
        def _():
            own_terms[rows, :] = stacked

        @pl.when(core != of_core)
        def _():
            other_terms[rows, :] = stacked.astype(BF)

    def put_second(ti, blocks):
        put(1, 18 - 9 * ti, blocks[::-1])

    weight_terms(wide_grad, odd_grad, hidden_turned, put_second)

    def backward(n, carry):
        grads = convolve(wide_grad, odd_grad, second_pairs, n)
        for q in range(SLOTS):
            m = SLOTS * n + q
            grad = grads[q * 512 : (q + 1) * 512] * slope[m]
            grad_turned[:, pl.ds(pl.multiple_of(m * 512, 512), 512)] = grad.astype(BF).T
        return carry

    lax.fori_loop(0, 4 // SLOTS, backward, 0, unroll=True)

    def put_first(ti, blocks):
        put(0, 9 * ti, [block.T for block in blocks])

    weight_terms(wide, odd, grad_turned, put_first)


def last_kernel(
    masked, hidden, links_in, occupied_in, second_in, g0, g1, g2, g3, g4,
    output,
    x, fx, fy, fz, wide, odd, pair_weights, second_weight, links, occupied, sems,
):
    copies = fetch(
        sems, (links_in, links), (occupied_in, occupied), (second_in, second_weight)
    )
    device = lax.axis_index(SPACE)
    faces = (fx, fy, fz)
    for n in range(4):
        x[n] = hidden[n].astype(F32)
    copies[0].wait()
    copies[1].wait()
    take_faces(x, links, device, (g0, g1, g2, g3, g4), 0, faces)
    copies[2].wait()
    lay_weights(pair_weights, lambda t: second_weight[t])

    def forward(n, carry):
        build(wide, odd, x, faces, [SLOTS * n + q for q in range(SLOTS)])
        seconds = convolve(wide, odd, pair_weights, n)
        for q in range(SLOTS):
            m = SLOTS * n + q
            keep = occupied[0, m].astype(F32)
            output[0, m] = ((masked[m] + seconds[q * 512 : (q + 1) * 512]) * keep).astype(BF)
        return carry

    lax.fori_loop(0, 4 // SLOTS, forward, 0, unroll=True)


def pair_kernel(own, other, terms, staged, sems):
    copies = []
    for q in range(8):
        rows = pl.ds(q * 448, 448)
        if q == 7:
            staged[pl.ds(3136, 320), :] = (own[pl.ds(3136, 320), :] + other[pl.ds(3136, 320), :].astype(F32)).astype(BF)
            staged[pl.ds(ROWS, 128), :] = jnp.zeros((128, 128), BF)
        else:
            staged[rows, :] = (own[rows, :] + other[rows, :].astype(F32)).astype(BF)
        copies.append(pltpu.make_async_copy(staged.at[rows], terms.at[rows], sems.at[q]))
        copies[-1].start()
    for copy in copies:
        copy.wait()


def sum_kernel(chunks, *rest):
    spread = rest[-1]
    total = chunks[0].astype(F32)

    def add(p, total):
        return total + chunks[p].astype(F32)

    total = lax.fori_loop(1, 64, add, total, unroll=7).astype(BF)

    def put(p, carry):
        spread[p] = total
        return carry

    lax.fori_loop(0, 64, put, 0, unroll=8)


def finish(core_of_first, source, outs, wide, sems):
    core = lax.axis_index("core")
    parts = 4
    rows = ROWS // parts
    for q in range(parts):
        at = pl.ds(q * rows, rows)
        wide[at, :] = source[at, :].astype(F32)
        for out, there in zip(outs, (core == core_of_first, core != core_of_first)):

            @pl.when(there)
            def _():
                pltpu.make_async_copy(wide.at[at], out.at[at], sems.at[q]).start()

    for q in range(parts):
        at = pl.ds(q * rows, rows)
        pltpu.make_async_copy(wide.at[at], outs[0].at[at], sems.at[q]).wait()


def finish_own_kernel(own, first_grad, second_grad, wide, sems):
    finish(0, own, (first_grad, second_grad), wide, sems)


def finish_other_kernel(other, first_in, second_in, first_grad, second_grad, wide, sems):
    finish(1, other, (first_grad, second_grad), wide, sems)


def send_shapes(fields):
    return tuple(jax.ShapeDtypeStruct((fields * w * 64, 128), BF) for w in (2, 2, 2, 2, 4))


def call(kernel, outs, ins, specs, scratch, limit, flops=0, nbytes=0, out_specs=VMEM, aliases={}):
    many = isinstance(outs, tuple)
    ins = [
        pltpu.with_memory_space_constraint(a, pltpu.HBM) if spec is HBM else a
        for a, spec in zip(ins, specs)
    ]
    return pl.pallas_call(
        kernel,
        out_shape=outs,
        in_specs=specs,
        out_specs=tuple(out_specs for _ in outs) if many else out_specs,
        scratch_shapes=scratch,
        input_output_aliases=aliases,
        compiler_params=pltpu.CompilerParams(vmem_limit_bytes=limit << 20),
        cost_estimate=pl.CostEstimate(flops=flops, bytes_accessed=nbytes, transcendentals=0),
    )(*ins)


def in_vmem(shape, dtype):
    return pltpu.VMEM(shape, dtype)


def step(voxels, occupied, neighbours, first_weight, second_weight, cotangent):
    field = pltpu.VMEM((4, 512, 128), F32)
    raw = pltpu.VMEM((1, 4, 512, 128), BF)
    links = pltpu.SMEM((1, 4, 6), jnp.int32)
    flags = pltpu.SMEM((1, 4), jnp.int32)
    weights = pltpu.VMEM((27, 128, 128), BF)
    sides = [pltpu.VMEM((4, 2, 64, 128), F32)] * 3
    padded = [pltpu.VMEM((3, 4, 10, 80, 128), BF), pltpu.VMEM((3, 4, 10, 64, 128), BF)]
    pairs = pltpu.VMEM((4608, 256), BF)
    turned = pltpu.VMEM((128, 2048), BF)
    sems = pltpu.SemaphoreType.DMA((5,))
    blocks = jax.ShapeDtypeStruct((4, 512, 128), BF)
    terms_shape = jax.ShapeDtypeStruct((ROWS, 128), F32)

    sent = call(
        first_faces_kernel,
        send_shapes(2),
        (voxels, cotangent, neighbours),
        [HBM] * 3,
        [field, field, raw, raw, links, sems],
        10,
        nbytes=2 << 20,
    )
    got = exchange(sent)
    prepared = call(
        prepare_kernel,
        (in_vmem((4, 512, 128), F32),) * 2 + (in_vmem((4608, 256), BF),) * 2,
        (voxels, cotangent, occupied, first_weight, second_weight),
        [HBM] * 5,
        [raw, raw, weights, weights, flags, sems],
        8,
        flops=1 << 20,
        nbytes=8 << 20,
    )
    hidden, own, other = call(
        main_kernel,
        (blocks, terms_shape, jax.ShapeDtypeStruct((ROWS, 128), BF)),
        tuple(prepared) + (neighbours, occupied) + got,
        [VMEM] * 4 + [HBM] * 2 + [VMEM] * 5,
        sides + sides + padded + padded + [field, turned, turned, links, flags, sems],
        26,
        flops=8 << 30,
        nbytes=8 << 20,
    )
    other = lax.ppermute(other, "core", PARTNER)
    chunks = jax.ShapeDtypeStruct((64 * CHUNK, 128), BF)
    terms = call(
        pair_kernel,
        chunks,
        (own, other),
        [VMEM] * 2,
        [pltpu.VMEM((64 * CHUNK, 128), BF), pltpu.SemaphoreType.DMA((8,))],
        4,
        nbytes=4 << 20,
        out_specs=HBM,
    )
    parts = lax.all_to_all(
        terms.reshape(64, CHUNK, 128), PEERS, split_axis=0, concat_axis=0, tiled=True
    )
    sent = call(
        hidden_faces_kernel,
        send_shapes(1),
        (hidden, neighbours),
        [VMEM, HBM],
        [field, links, sems],
        6,
        nbytes=1 << 20,
    )
    got = exchange(sent)
    spread = call(
        sum_kernel,
        jax.ShapeDtypeStruct((64, CHUNK, 128), BF),
        (parts,) + tuple(sent),
        [VMEM] + [ANY] * 5,
        [],
        6,
        nbytes=2 << 20,
    )
    mine = lax.all_to_all(spread, PEERS, split_axis=0, concat_axis=0, tiled=True)
    output = call(
        last_kernel,
        jax.ShapeDtypeStruct((1, 4, 512, 128), BF),
        (prepared[0], hidden, neighbours, occupied, second_weight) + got,
        [VMEM] * 2 + [HBM] * 3 + [VMEM] * 5,
        [field] + sides + padded + [pairs, weights, links, flags, sems],
        20,
        flops=3 << 30,
        nbytes=4 << 20,
    )
    mine, output = lax.optimization_barrier((mine, output))
    mine = mine.reshape(64 * CHUNK, 128)
    theirs = lax.ppermute(mine, "core", PARTNER)
    wide = pltpu.VMEM((ROWS, 128), F32)
    grads = call(
        finish_own_kernel, (terms_shape, terms_shape), (mine,), [VMEM], [wide, sems], 4, nbytes=3 << 20, out_specs=HBM
    )
    first_grad, second_grad = call(
        finish_other_kernel,
        (terms_shape, terms_shape),
        (theirs,) + tuple(grads),
        [VMEM, HBM, HBM],
        [wide, sems],
        4,
        nbytes=3 << 20,
        out_specs=HBM,
        aliases={1: 0, 2: 1},
    )
    return output, first_grad.reshape(27, 128, 128), second_grad.reshape(27, 128, 128)


def solution(mesh):
    mesh = jax.sharding.Mesh(mesh.devices.reshape(4, 4, 2, 4), ("z", "x", "core", "rep"))
    placed = (
        P("rep", SPACE, None, None),
        P("rep", SPACE),
        P("rep", SPACE, None),
        P(),
        P(),
        P("rep", SPACE, None, None),
    )
    return jax.shard_map(
        step,
        mesh=mesh,
        in_specs=placed,
        out_specs=(P("rep", SPACE, None, None), P(), P()),
        check_vma=False,
    )
```

```python
import jax
import jax.numpy as jnp
from jax import lax
from jax.experimental import pallas as pl
from jax.experimental.pallas import tpu as pltpu
from jax.sharding import PartitionSpec as P


BF = jnp.bfloat16
F32 = jnp.float32
VMEM = pl.BlockSpec(memory_space=pltpu.VMEM)
HBM = pl.BlockSpec(memory_space=pltpu.HBM)
ANY = pl.BlockSpec(memory_space=pl.ANY)
ROWS = 3456
SLOTS = 2
CHUNK = 56


def tile_of(s):
    return (s & 1) | ((s >> 1) & 2), ((s >> 1) & 1) | ((s >> 2) & 2), s >> 4


def owner_of(a, b, z):
    return (a & 1) | ((b & 1) << 1) | ((a >> 1) << 2) | ((b >> 1) << 3) | (z << 4)


def swaps(kind):
    pairs = []
    for s in range(32):
        a, b, z = tile_of(s)
        if kind == "xe":
            a ^= 1
        elif kind == "ye":
            b ^= 1
        elif kind == "z":
            z ^= 1
        elif kind == "xo":
            a = 3 - a
        elif kind == "yo":
            b = 3 - b
        pairs.append((s, owner_of(a, b, z)))
    return pairs


SWAPS = tuple(swaps(kind) for kind in ("xe", "xo", "ye", "yo", "z"))


SPACE = ("z", "x", "core")
PEERS = ("x", "rep", "z")
PARTNER = ((0, 1), (1, 0))


def exchange(sent):
    got = []
    for way in range(5):
        got.append(lax.ppermute(sent[way], SPACE, SWAPS[way]))
    return tuple(got)


def remote_links(links, face, device):
    found = []
    for n in range(4):
        link = links[0, n, face]
        valid = link >= 0
        found.append((link, valid, valid & ((link >> 2) != device)))
    return found


def face_of(x, n, axis, layer):
    if axis == 0:
        return x[n, pl.ds(layer * 64, 64), :]
    if axis == 1:
        return jnp.concatenate([x[n, pl.ds(i * 64 + layer * 8, 8), :] for i in range(8)], axis=0)
    return x[n, pl.ds(layer, 64, stride=8), :]


def pack_faces(fields, links, device, sends):
    bits = (device & 1, (device >> 1) & 1, device >> 4)
    for axis in range(3):
        width = 4 if axis == 2 else 2
        for odd in range(1 if axis == 2 else 2):
            send = sends[2 * axis + odd]
            side = bits[axis] ^ (1 - odd)
            rank = jnp.int32(0)
            for n in range(4):
                link = links[0, n, 2 * axis + side]
                remote = (link >= 0) & ((link >> 2) != device)
                at = rank

                @pl.when(remote)
                def _():
                    for a, x in enumerate(fields):
                        row = pl.multiple_of((a * width + at) * 64, 64)
                        send[pl.ds(row, 64), :] = face_of(x, n, axis, side * 7).astype(BF)

                rank = rank + remote.astype(jnp.int32)


def take_faces(x, links, device, got, field, faces):
    bits = (device & 1, (device >> 1) & 1, device >> 4)
    for axis in range(3):
        width = 4 if axis == 2 else 2
        for side in range(2):
            found = remote_links(links, 2 * axis + side, device)
            for n in range(4):
                link, valid, remote = found[n]
                slot = link & 3
                rank = jnp.int32(0)
                for q in range(4):
                    if q != n:
                        lower = found[q][2] & ((found[q][0] & 3) < slot)
                        rank = rank + lower.astype(jnp.int32)
                rank = jnp.minimum(jnp.where(remote, rank, 0), width - 1)
                row = pl.ds(pl.multiple_of((field * width + rank) * 64, 64), 64)
                if axis == 2:
                    far = got[4][row, :].astype(F32)
                    value = jnp.where(remote, far, 0.0)
                else:
                    even = (bits[axis] ^ side) == 1
                    far = jnp.where(even, got[2 * axis][row, :], got[2 * axis + 1][row, :])
                    near = face_of(x, jnp.where(valid, slot, 0), axis, 0 if side else 7)
                    value = jnp.where(valid, jnp.where(remote, far.astype(F32), near), 0.0)
                faces[axis][n, side] = value


def build(wide, odd, x, faces, slots):
    k_of = lax.broadcasted_iota(jnp.int32, (10, 8, 128), 1)
    at_low, at_high = k_of == 0, k_of == 7
    none = jnp.zeros((1, 8, 128), F32)

    def block(n):
        for i in range(10):
            if i in (0, 9):
                core = faces[0][n, 0 if i == 0 else 1].reshape(8, 8, 128)
                layers = jnp.concatenate((none, core, none), axis=0)
                low, high = jnp.zeros_like(layers), jnp.zeros_like(layers)
            else:
                at = pl.ds((i - 1) * 8, 8)
                core = x[n, pl.ds((i - 1) * 64, 64), :].reshape(8, 8, 128)
                layers = jnp.concatenate(
                    (faces[1][n, 0, at, :][None], core, faces[1][n, 1, at, :][None]), axis=0
                )
                low, high = (
                    jnp.concatenate(
                        (none, jnp.broadcast_to(faces[2][n, side, at, :][:, None, :], (8, 8, 128)), none),
                        axis=0,
                    )
                    for side in range(2)
                )
            before = jnp.where(at_low, low, pltpu.roll(layers, 1, 1))
            after = jnp.where(at_high, high, pltpu.roll(layers, 7, 1))
            for tk, shifted in enumerate((before, layers, after)):
                wide[tk, n, i] = shifted.reshape(80, 128).astype(BF)
                odd[tk, n, i] = shifted[1:9].reshape(64, 128).astype(BF)

    for n in slots:
        block(n)


def tap(wide, odd, n, i, tj, tk):
    if tj == 1:
        return odd[tk, n, i]
    return wide[tk, n, i, pl.ds(8 * tj, 64), :]


def convolve(wide, odd, pair_weights, n):
    columns = []
    for layer in range(4):
        for tj in range(3):
            for tk in range(3):
                columns.append(
                    jnp.concatenate([tap(wide, odd, SLOTS * n + q, 2 * p + layer, tj, tk) for q in range(SLOTS) for p in range(4)], axis=0)
                )
    group = jnp.concatenate(columns, axis=1)
    both = jnp.dot(group, pair_weights[...], preferred_element_type=F32)
    rows = []
    for p in range(4 * SLOTS):
        for half in range(2):
            rows.append(both[p * 64 : (p + 1) * 64, half * 128 : (half + 1) * 128])
    return jnp.concatenate(rows, axis=0)


def lay_weights(pair_weights, block_of):
    pair_weights[pl.ds(3456, 1152), pl.ds(0, 128)] = jnp.zeros((1152, 128), BF)
    pair_weights[pl.ds(0, 1152), pl.ds(128, 128)] = jnp.zeros((1152, 128), BF)
    for t in range(27):
        block = block_of(t)
        pair_weights[pl.ds(t * 128, 128), pl.ds(0, 128)] = block
        pair_weights[pl.ds((t + 9) * 128, 128), pl.ds(128, 128)] = block


GROUP = 16


def weight_terms(wide, odd, turned, put):
    for start in range(0, 27, GROUP):
        taps = range(start, min(start + GROUP, 27))
        columns = [
            jnp.concatenate(
                [tap(wide, odd, n, i + t // 9, t // 3 % 3, t % 3) for n in range(4) for i in range(8)], axis=0
            )
            for t in taps
        ]
        total = jnp.dot(turned[...], jnp.concatenate(columns, axis=1), preferred_element_type=F32)
        put(start, [total[:, q * 128 : (q + 1) * 128] for q in range(len(taps))])


def fetch(sems, *pairs):
    copies = [pltpu.make_async_copy(a, b, sems.at[q]) for q, (a, b) in enumerate(pairs)]
    for copy in copies:
        copy.start()
    return copies


def first_faces_kernel(voxels, cotangent, links_in, *rest):
    sends, (x, g, raw_x, raw_g, links, sems) = rest[:5], rest[5:]
    device = lax.axis_index(SPACE)
    copies = fetch(sems, (links_in, links), (voxels, raw_x), (cotangent, raw_g))
    for copy, raw, wide in ((copies[1], raw_x, x), (copies[2], raw_g, g)):
        copy.wait()
        for n in range(4):
            wide[n] = raw[0, n].astype(F32)
    copies[0].wait()
    pack_faces((x, g), links, device, sends)


def prepare_kernel(
    voxels, cotangent, occupied_in, first_in, second_in,
    x, g, first_pairs, second_pairs,
    raw_x, raw_g, first_weight, second_weight, occupied, sems,
):
    copies = fetch(
        sems,
        (occupied_in, occupied),
        (voxels, raw_x),
        (cotangent, raw_g),
        (first_in, first_weight),
        (second_in, second_weight),
    )
    copies[0].wait()
    for copy, raw, wide in ((copies[1], raw_x, x), (copies[2], raw_g, g)):
        copy.wait()
        for n in range(4):
            wide[n] = raw[0, n].astype(F32) * occupied[0, n].astype(F32)
    copies[3].wait()
    lay_weights(first_pairs, lambda t: first_weight[t])
    copies[4].wait()
    lay_weights(second_pairs, lambda t: second_weight[26 - t].T)


def hidden_faces_kernel(hidden, links_in, *rest):
    sends, (x, links, sems) = rest[:5], rest[5:]
    device = lax.axis_index(SPACE)
    copies = fetch(sems, (links_in, links))
    for n in range(4):
        x[n] = hidden[n].astype(F32)
    copies[0].wait()
    pack_faces((x,), links, device, sends)


def main_kernel(
    x, g, first_pairs, second_pairs, links_in, occupied_in, g0, g1, g2, g3, g4,
    hidden, own_terms, other_terms,
    fx, fy, fz, gx, gy, gz, wide, odd, wide_grad, odd_grad, slope, hidden_turned, grad_turned, links, occupied, sems,
):
    copies = fetch(sems, (links_in, links), (occupied_in, occupied))
    device = lax.axis_index(SPACE)
    got = (g0, g1, g2, g3, g4)
    faces = (fx, fy, fz)
    copies[0].wait()
    copies[1].wait()
    take_faces(x, links, device, got, 0, faces)
    take_faces(g, links, device, got, 1, (gx, gy, gz))

    def forward(n, carry):
        slots = [SLOTS * n + q for q in range(SLOTS)]
        build(wide, odd, x, faces, slots)
        build(wide_grad, odd_grad, g, (gx, gy, gz), slots)
        firsts = convolve(wide, odd, first_pairs, n)
        for q in range(SLOTS):
            m = SLOTS * n + q
            keep = occupied[0, m].astype(F32)
            first = firsts[q * 512 : (q + 1) * 512]
            sigma = jax.nn.sigmoid(first)
            value = (first * sigma * keep).astype(BF)
            hidden[m] = value
            hidden_turned[:, pl.ds(pl.multiple_of(m * 512, 512), 512)] = value.T
            slope[m] = sigma * (1.0 + first * (1.0 - sigma)) * keep
        return carry

    lax.fori_loop(0, 4 // SLOTS, forward, 0, unroll=True)


    core = device & 1

    def put(of_core, start, blocks):
        rows = pl.ds(start * 128, 128 * len(blocks))
        stacked = jnp.concatenate(blocks, axis=0)

        @pl.when(core == of_core)
        def _():
            own_terms[rows, :] = stacked

        @pl.when(core != of_core)
        def _():
            other_terms[rows, :] = stacked.astype(BF)

    def put_second(start, blocks):
        put(1, 27 - start - len(blocks), blocks[::-1])

    weight_terms(wide_grad, odd_grad, hidden_turned, put_second)

    def backward(n, carry):
        grads = convolve(wide_grad, odd_grad, second_pairs, n)
        for q in range(SLOTS):
            m = SLOTS * n + q
            grad = grads[q * 512 : (q + 1) * 512] * slope[m]
            grad_turned[:, pl.ds(pl.multiple_of(m * 512, 512), 512)] = grad.astype(BF).T
        return carry

    lax.fori_loop(0, 4 // SLOTS, backward, 0, unroll=True)

    def put_first(start, blocks):
        put(0, start, [block.T for block in blocks])

    weight_terms(wide, odd, grad_turned, put_first)


def last_kernel(
    masked, hidden, links_in, occupied_in, second_in, g0, g1, g2, g3, g4,
    output,
    x, fx, fy, fz, wide, odd, pair_weights, second_weight, links, occupied, sems,
):
    copies = fetch(
        sems, (links_in, links), (occupied_in, occupied), (second_in, second_weight)
    )
    device = lax.axis_index(SPACE)
    faces = (fx, fy, fz)
    for n in range(4):
        x[n] = hidden[n].astype(F32)
    copies[0].wait()
    copies[1].wait()
    take_faces(x, links, device, (g0, g1, g2, g3, g4), 0, faces)
    copies[2].wait()
    lay_weights(pair_weights, lambda t: second_weight[t])

    def forward(n, carry):
        build(wide, odd, x, faces, [SLOTS * n + q for q in range(SLOTS)])
        seconds = convolve(wide, odd, pair_weights, n)
        for q in range(SLOTS):
            m = SLOTS * n + q
            keep = occupied[0, m].astype(F32)
            output[0, m] = ((masked[m] + seconds[q * 512 : (q + 1) * 512]) * keep).astype(BF)
        return carry

    lax.fori_loop(0, 4 // SLOTS, forward, 0, unroll=True)


def pair_kernel(own, other, terms, staged, sems):
    copies = []
    for q in range(8):
        rows = pl.ds(q * 448, 448)
        if q == 7:
            staged[pl.ds(3136, 320), :] = (own[pl.ds(3136, 320), :] + other[pl.ds(3136, 320), :].astype(F32)).astype(BF)
            staged[pl.ds(ROWS, 128), :] = jnp.zeros((128, 128), BF)
        else:
            staged[rows, :] = (own[rows, :] + other[rows, :].astype(F32)).astype(BF)
        copies.append(pltpu.make_async_copy(staged.at[rows], terms.at[rows], sems.at[q]))
        copies[-1].start()
    for copy in copies:
        copy.wait()


def sum_kernel(chunks, *rest):
    spread = rest[-1]
    total = chunks[0].astype(F32)

    def add(p, total):
        return total + chunks[p].astype(F32)

    total = lax.fori_loop(1, 64, add, total, unroll=7).astype(BF)

    def put(p, carry):
        spread[p] = total
        return carry

    lax.fori_loop(0, 64, put, 0, unroll=8)


def finish(core_of_first, source, outs, wide, sems):
    core = lax.axis_index("core")
    parts = 4
    rows = ROWS // parts
    for q in range(parts):
        at = pl.ds(q * rows, rows)
        wide[at, :] = source[at, :].astype(F32)
        for out, there in zip(outs, (core == core_of_first, core != core_of_first)):

            @pl.when(there)
            def _():
                pltpu.make_async_copy(wide.at[at], out.at[at], sems.at[q]).start()

    for q in range(parts):
        at = pl.ds(q * rows, rows)
        pltpu.make_async_copy(wide.at[at], outs[0].at[at], sems.at[q]).wait()


def finish_own_kernel(own, first_grad, second_grad, wide, sems):
    finish(0, own, (first_grad, second_grad), wide, sems)


def finish_other_kernel(other, first_in, second_in, first_grad, second_grad, wide, sems):
    finish(1, other, (first_grad, second_grad), wide, sems)


def send_shapes(fields):
    return tuple(jax.ShapeDtypeStruct((fields * w * 64, 128), BF) for w in (2, 2, 2, 2, 4))


def call(kernel, outs, ins, specs, scratch, limit, flops=0, nbytes=0, out_specs=VMEM, aliases={}):
    many = isinstance(outs, tuple)
    ins = [
        pltpu.with_memory_space_constraint(a, pltpu.HBM) if spec is HBM else a
        for a, spec in zip(ins, specs)
    ]
    return pl.pallas_call(
        kernel,
        out_shape=outs,
        in_specs=specs,
        out_specs=tuple(out_specs for _ in outs) if many else out_specs,
        scratch_shapes=scratch,
        input_output_aliases=aliases,
        compiler_params=pltpu.CompilerParams(vmem_limit_bytes=limit << 20),
        cost_estimate=pl.CostEstimate(flops=flops, bytes_accessed=nbytes, transcendentals=0),
    )(*ins)


def in_vmem(shape, dtype):
    return pltpu.VMEM(shape, dtype)


def step(voxels, occupied, neighbours, first_weight, second_weight, cotangent):
    field = pltpu.VMEM((4, 512, 128), F32)
    raw = pltpu.VMEM((1, 4, 512, 128), BF)
    links = pltpu.SMEM((1, 4, 6), jnp.int32)
    flags = pltpu.SMEM((1, 4), jnp.int32)
    weights = pltpu.VMEM((27, 128, 128), BF)
    sides = [pltpu.VMEM((4, 2, 64, 128), F32)] * 3
    padded = [pltpu.VMEM((3, 4, 10, 80, 128), BF), pltpu.VMEM((3, 4, 10, 64, 128), BF)]
    pairs = pltpu.VMEM((4608, 256), BF)
    turned = pltpu.VMEM((128, 2048), BF)
    sems = pltpu.SemaphoreType.DMA((5,))
    blocks = jax.ShapeDtypeStruct((4, 512, 128), BF)
    terms_shape = jax.ShapeDtypeStruct((ROWS, 128), F32)

    sent = call(
        first_faces_kernel,
        send_shapes(2),
        (voxels, cotangent, neighbours),
        [HBM] * 3,
        [field, field, raw, raw, links, sems],
        10,
        nbytes=2 << 20,
    )
    got = exchange(sent)
    prepared = call(
        prepare_kernel,
        (in_vmem((4, 512, 128), F32),) * 2 + (in_vmem((4608, 256), BF),) * 2,
        (voxels, cotangent, occupied, first_weight, second_weight),
        [HBM] * 5,
        [raw, raw, weights, weights, flags, sems],
        8,
        flops=1 << 20,
        nbytes=8 << 20,
    )
    hidden, own, other = call(
        main_kernel,
        (blocks, terms_shape, jax.ShapeDtypeStruct((ROWS, 128), BF)),
        tuple(prepared) + (neighbours, occupied) + got,
        [VMEM] * 4 + [HBM] * 2 + [VMEM] * 5,
        sides + sides + padded + padded + [field, turned, turned, links, flags, sems],
        26,
        flops=8 << 30,
        nbytes=8 << 20,
    )
    other = lax.ppermute(other, "core", PARTNER)
    chunks = jax.ShapeDtypeStruct((64 * CHUNK, 128), BF)
    terms = call(
        pair_kernel,
        chunks,
        (own, other),
        [VMEM] * 2,
        [pltpu.VMEM((64 * CHUNK, 128), BF), pltpu.SemaphoreType.DMA((8,))],
        4,
        nbytes=4 << 20,
        out_specs=HBM,
    )
    parts = lax.all_to_all(
        terms.reshape(64, CHUNK, 128), PEERS, split_axis=0, concat_axis=0, tiled=True
    )
    sent = call(
        hidden_faces_kernel,
        send_shapes(1),
        (hidden, neighbours),
        [VMEM, HBM],
        [field, links, sems],
        6,
        nbytes=1 << 20,
    )
    got = exchange(sent)
    spread = call(
        sum_kernel,
        jax.ShapeDtypeStruct((64, CHUNK, 128), BF),
        (parts,) + tuple(sent),
        [VMEM] + [ANY] * 5,
        [],
        6,
        nbytes=2 << 20,
    )
    mine = lax.all_to_all(spread, PEERS, split_axis=0, concat_axis=0, tiled=True)
    output = call(
        last_kernel,
        jax.ShapeDtypeStruct((1, 4, 512, 128), BF),
        (prepared[0], hidden, neighbours, occupied, second_weight) + got,
        [VMEM] * 2 + [HBM] * 3 + [VMEM] * 5,
        [field] + sides + padded + [pairs, weights, links, flags, sems],
        20,
        flops=3 << 30,
        nbytes=4 << 20,
    )
    mine, output = lax.optimization_barrier((mine, output))
    mine = mine.reshape(64 * CHUNK, 128)
    theirs = lax.ppermute(mine, "core", PARTNER)
    wide = pltpu.VMEM((ROWS, 128), F32)
    grads = call(
        finish_own_kernel, (terms_shape, terms_shape), (mine,), [VMEM], [wide, sems], 4, nbytes=3 << 20, out_specs=HBM
    )
    first_grad, second_grad = call(
        finish_other_kernel,
        (terms_shape, terms_shape),
        (theirs,) + tuple(grads),
        [VMEM, HBM, HBM],
        [wide, sems],
        4,
        nbytes=3 << 20,
        out_specs=HBM,
        aliases={1: 0, 2: 1},
    )
    return output, first_grad.reshape(27, 128, 128), second_grad.reshape(27, 128, 128)


def solution(mesh):
    mesh = jax.sharding.Mesh(mesh.devices.reshape(4, 4, 2, 4), ("z", "x", "core", "rep"))
    placed = (
        P("rep", SPACE, None, None),
        P("rep", SPACE),
        P("rep", SPACE, None),
        P(),
        P(),
        P("rep", SPACE, None, None),
    )
    return jax.shard_map(
        step,
        mesh=mesh,
        in_specs=placed,
        out_specs=(P("rep", SPACE, None, None), P(), P()),
        check_vma=False,
    )
```

```python
import jax
import jax.numpy as jnp
from jax import lax
from jax.experimental import pallas as pl
from jax.experimental.pallas import tpu as pltpu
from jax.sharding import PartitionSpec as P


BF = jnp.bfloat16
F32 = jnp.float32
VMEM = pl.BlockSpec(memory_space=pltpu.VMEM)
HBM = pl.BlockSpec(memory_space=pltpu.HBM)
ANY = pl.BlockSpec(memory_space=pl.ANY)
ROWS = 3456
SLOTS = 2
CHUNK = 56


def tile_of(s):
    return (s & 1) | ((s >> 1) & 2), ((s >> 1) & 1) | ((s >> 2) & 2), s >> 4


def owner_of(a, b, z):
    return (a & 1) | ((b & 1) << 1) | ((a >> 1) << 2) | ((b >> 1) << 3) | (z << 4)


def swaps(kind):
    pairs = []
    for s in range(32):
        a, b, z = tile_of(s)
        if kind == "xe":
            a ^= 1
        elif kind == "ye":
            b ^= 1
        elif kind == "z":
            z ^= 1
        elif kind == "xo":
            a = 3 - a
        elif kind == "yo":
            b = 3 - b
        pairs.append((s, owner_of(a, b, z)))
    return pairs


SWAPS = tuple(swaps(kind) for kind in ("xe", "xo", "ye", "yo", "z"))


SPACE = ("z", "x", "core")
PEERS = ("x", "rep", "z")
PARTNER = ((0, 1), (1, 0))


def exchange(sent):
    got = []
    for way in range(5):
        got.append(lax.ppermute(sent[way], SPACE, SWAPS[way]))
    return tuple(got)


def remote_links(links, face, device):
    found = []
    for n in range(4):
        link = links[0, n, face]
        valid = link >= 0
        found.append((link, valid, valid & ((link >> 2) != device)))
    return found


def face_of(x, n, axis, layer):
    if axis == 0:
        return x[n, pl.ds(layer * 64, 64), :]
    if axis == 1:
        return jnp.concatenate([x[n, pl.ds(i * 64 + layer * 8, 8), :] for i in range(8)], axis=0)
    return x[n, pl.ds(layer, 64, stride=8), :]


def pack_faces(fields, links, device, sends):
    bits = (device & 1, (device >> 1) & 1, device >> 4)
    for axis in range(3):
        width = 4 if axis == 2 else 2
        for odd in range(1 if axis == 2 else 2):
            send = sends[2 * axis + odd]
            side = bits[axis] ^ (1 - odd)
            rank = jnp.int32(0)
            for n in range(4):
                link = links[0, n, 2 * axis + side]
                remote = (link >= 0) & ((link >> 2) != device)
                at = jnp.minimum(rank, width - 1)
                for a, x in enumerate(fields):
                    row = pl.ds(pl.multiple_of((a * width + at) * 64, 64), 64)
                    face = face_of(x, n, axis, side * 7).astype(BF)
                    send[row, :] = jnp.where(remote, face, send[row, :])
                rank = rank + remote.astype(jnp.int32)


def take_faces(x, links, device, got, field, faces):
    bits = (device & 1, (device >> 1) & 1, device >> 4)
    for axis in range(3):
        width = 4 if axis == 2 else 2
        for side in range(2):
            found = remote_links(links, 2 * axis + side, device)
            for n in range(4):
                link, valid, remote = found[n]
                slot = link & 3
                rank = jnp.int32(0)
                for q in range(4):
                    if q != n:
                        lower = found[q][2] & ((found[q][0] & 3) < slot)
                        rank = rank + lower.astype(jnp.int32)
                rank = jnp.minimum(jnp.where(remote, rank, 0), width - 1)
                row = pl.ds(pl.multiple_of((field * width + rank) * 64, 64), 64)
                if axis == 2:
                    far = got[4][row, :].astype(F32)
                    value = jnp.where(remote, far, 0.0)
                else:
                    even = (bits[axis] ^ side) == 1
                    far = jnp.where(even, got[2 * axis][row, :], got[2 * axis + 1][row, :])
                    near = face_of(x, jnp.where(valid, slot, 0), axis, 0 if side else 7)
                    value = jnp.where(valid, jnp.where(remote, far.astype(F32), near), 0.0)
                faces[axis][n, side] = value


def build(wide, odd, x, faces, slots):
    k_of = lax.broadcasted_iota(jnp.int32, (10, 8, 128), 1)
    at_low, at_high = k_of == 0, k_of == 7
    none = jnp.zeros((1, 8, 128), F32)

    def block(n):
        for i in range(10):
            if i in (0, 9):
                core = faces[0][n, 0 if i == 0 else 1].reshape(8, 8, 128)
                layers = jnp.concatenate((none, core, none), axis=0)
                low, high = jnp.zeros_like(layers), jnp.zeros_like(layers)
            else:
                at = pl.ds((i - 1) * 8, 8)
                core = x[n, pl.ds((i - 1) * 64, 64), :].reshape(8, 8, 128)
                layers = jnp.concatenate(
                    (faces[1][n, 0, at, :][None], core, faces[1][n, 1, at, :][None]), axis=0
                )
                low, high = (
                    jnp.concatenate(
                        (none, jnp.broadcast_to(faces[2][n, side, at, :][:, None, :], (8, 8, 128)), none),
                        axis=0,
                    )
                    for side in range(2)
                )
            before = jnp.where(at_low, low, pltpu.roll(layers, 1, 1))
            after = jnp.where(at_high, high, pltpu.roll(layers, 7, 1))
            for tk, shifted in enumerate((before, layers, after)):
                wide[tk, n, i] = shifted.reshape(80, 128).astype(BF)
                odd[tk, n, i] = shifted[1:9].reshape(64, 128).astype(BF)

    for n in slots:
        block(n)


def tap(wide, odd, n, i, tj, tk):
    if tj == 1:
        return odd[tk, n, i]
    return wide[tk, n, i, pl.ds(8 * tj, 64), :]


def convolve(wide, odd, pair_weights, n):
    columns = []
    for layer in range(4):
        for tj in range(3):
            for tk in range(3):
                columns.append(
                    jnp.concatenate([tap(wide, odd, SLOTS * n + q, 2 * p + layer, tj, tk) for q in range(SLOTS) for p in range(4)], axis=0)
                )
    group = jnp.concatenate(columns, axis=1)
    both = jnp.dot(group, pair_weights[...], preferred_element_type=F32)
    rows = []
    for p in range(4 * SLOTS):
        for half in range(2):
            rows.append(both[p * 64 : (p + 1) * 64, half * 128 : (half + 1) * 128])
    return jnp.concatenate(rows, axis=0)


def lay_weights(pair_weights, block_of):
    pair_weights[pl.ds(3456, 1152), pl.ds(0, 128)] = jnp.zeros((1152, 128), BF)
    pair_weights[pl.ds(0, 1152), pl.ds(128, 128)] = jnp.zeros((1152, 128), BF)
    for t in range(27):
        block = block_of(t)
        pair_weights[pl.ds(t * 128, 128), pl.ds(0, 128)] = block
        pair_weights[pl.ds((t + 9) * 128, 128), pl.ds(128, 128)] = block


GROUP = 16


def weight_terms(wide, odd, turned, put):
    for start in range(0, 27, GROUP):
        taps = range(start, min(start + GROUP, 27))
        columns = [
            jnp.concatenate(
                [tap(wide, odd, n, i + t // 9, t // 3 % 3, t % 3) for n in range(4) for i in range(8)], axis=0
            )
            for t in taps
        ]
        total = jnp.dot(turned[...], jnp.concatenate(columns, axis=1), preferred_element_type=F32)
        put(start, [total[:, q * 128 : (q + 1) * 128] for q in range(len(taps))])


def fetch(sems, *pairs):
    copies = [pltpu.make_async_copy(a, b, sems.at[q]) for q, (a, b) in enumerate(pairs)]
    for copy in copies:
        copy.start()
    return copies


def first_faces_kernel(voxels, cotangent, links_in, *rest):
    sends, (x, g, raw_x, raw_g, links, sems) = rest[:5], rest[5:]
    device = lax.axis_index(SPACE)
    copies = fetch(sems, (links_in, links), (voxels, raw_x), (cotangent, raw_g))
    for copy, raw, wide in ((copies[1], raw_x, x), (copies[2], raw_g, g)):
        copy.wait()
        for n in range(4):
            wide[n] = raw[0, n].astype(F32)
    copies[0].wait()
    pack_faces((x, g), links, device, sends)


def prepare_kernel(
    voxels, cotangent, occupied_in, first_in, second_in,
    x, g, first_pairs, second_pairs,
    raw_x, raw_g, first_weight, second_weight, occupied, sems,
):
    copies = fetch(
        sems,
        (occupied_in, occupied),
        (voxels, raw_x),
        (cotangent, raw_g),
        (first_in, first_weight),
        (second_in, second_weight),
    )
    copies[0].wait()
    for copy, raw, wide in ((copies[1], raw_x, x), (copies[2], raw_g, g)):
        copy.wait()
        for n in range(4):
            wide[n] = raw[0, n].astype(F32) * occupied[0, n].astype(F32)
    copies[3].wait()
    lay_weights(first_pairs, lambda t: first_weight[t])
    copies[4].wait()
    lay_weights(second_pairs, lambda t: second_weight[26 - t].T)


def hidden_faces_kernel(hidden, links_in, *rest):
    sends, (x, links, sems) = rest[:5], rest[5:]
    device = lax.axis_index(SPACE)
    copies = fetch(sems, (links_in, links))
    for n in range(4):
        x[n] = hidden[n].astype(F32)
    copies[0].wait()
    pack_faces((x,), links, device, sends)


def main_kernel(
    x, g, first_pairs, second_pairs, links_in, occupied_in, g0, g1, g2, g3, g4,
    hidden, own_terms, other_terms,
    fx, fy, fz, gx, gy, gz, wide, odd, wide_grad, odd_grad, slope, hidden_turned, grad_turned, links, occupied, sems,
):
    copies = fetch(sems, (links_in, links), (occupied_in, occupied))
    device = lax.axis_index(SPACE)
    got = (g0, g1, g2, g3, g4)
    faces = (fx, fy, fz)
    copies[0].wait()
    copies[1].wait()
    take_faces(x, links, device, got, 0, faces)
    take_faces(g, links, device, got, 1, (gx, gy, gz))

    def forward(n, carry):
        slots = [SLOTS * n + q for q in range(SLOTS)]
        build(wide, odd, x, faces, slots)
        build(wide_grad, odd_grad, g, (gx, gy, gz), slots)
        firsts = convolve(wide, odd, first_pairs, n)
        for q in range(SLOTS):
            m = SLOTS * n + q
            keep = occupied[0, m].astype(F32)
            first = firsts[q * 512 : (q + 1) * 512]
            sigma = jax.nn.sigmoid(first)
            value = (first * sigma * keep).astype(BF)
            hidden[m] = value
            hidden_turned[:, pl.ds(pl.multiple_of(m * 512, 512), 512)] = value.T
            slope[m] = sigma * (1.0 + first * (1.0 - sigma)) * keep
        return carry

    lax.fori_loop(0, 4 // SLOTS, forward, 0, unroll=True)


    core = device & 1

    def put(of_core, start, blocks):
        rows = pl.ds(start * 128, 128 * len(blocks))
        stacked = jnp.concatenate(blocks, axis=0)

        @pl.when(core == of_core)
        def _():
            own_terms[rows, :] = stacked

        @pl.when(core != of_core)
        def _():
            other_terms[rows, :] = stacked.astype(BF)

    def put_second(start, blocks):
        put(1, 27 - start - len(blocks), blocks[::-1])

    weight_terms(wide_grad, odd_grad, hidden_turned, put_second)

    def backward(n, carry):
        grads = convolve(wide_grad, odd_grad, second_pairs, n)
        for q in range(SLOTS):
            m = SLOTS * n + q
            grad = grads[q * 512 : (q + 1) * 512] * slope[m]
            grad_turned[:, pl.ds(pl.multiple_of(m * 512, 512), 512)] = grad.astype(BF).T
        return carry

    lax.fori_loop(0, 4 // SLOTS, backward, 0, unroll=True)

    def put_first(start, blocks):
        put(0, start, [block.T for block in blocks])

    weight_terms(wide, odd, grad_turned, put_first)


def last_kernel(
    masked, hidden, links_in, occupied_in, second_in, g0, g1, g2, g3, g4,
    output,
    x, fx, fy, fz, wide, odd, pair_weights, second_weight, links, occupied, sems,
):
    copies = fetch(
        sems, (links_in, links), (occupied_in, occupied), (second_in, second_weight)
    )
    device = lax.axis_index(SPACE)
    faces = (fx, fy, fz)
    for n in range(4):
        x[n] = hidden[n].astype(F32)
    copies[0].wait()
    copies[1].wait()
    take_faces(x, links, device, (g0, g1, g2, g3, g4), 0, faces)
    copies[2].wait()
    lay_weights(pair_weights, lambda t: second_weight[t])

    def forward(n, carry):
        build(wide, odd, x, faces, [SLOTS * n + q for q in range(SLOTS)])
        seconds = convolve(wide, odd, pair_weights, n)
        for q in range(SLOTS):
            m = SLOTS * n + q
            keep = occupied[0, m].astype(F32)
            output[0, m] = ((masked[m] + seconds[q * 512 : (q + 1) * 512]) * keep).astype(BF)
        return carry

    lax.fori_loop(0, 4 // SLOTS, forward, 0, unroll=True)


def pair_kernel(own, other, terms, staged, sems):
    copies = []
    for q in range(8):
        rows = pl.ds(q * 448, 448)
        if q == 7:
            staged[pl.ds(3136, 320), :] = (own[pl.ds(3136, 320), :] + other[pl.ds(3136, 320), :].astype(F32)).astype(BF)
            staged[pl.ds(ROWS, 128), :] = jnp.zeros((128, 128), BF)
        else:
            staged[rows, :] = (own[rows, :] + other[rows, :].astype(F32)).astype(BF)
        copies.append(pltpu.make_async_copy(staged.at[rows], terms.at[rows], sems.at[q]))
        copies[-1].start()
    for copy in copies:
        copy.wait()


def sum_kernel(chunks, *rest):
    spread = rest[-1]
    total = chunks[0].astype(F32)

    def add(p, total):
        return total + chunks[p].astype(F32)

    total = lax.fori_loop(1, 64, add, total, unroll=7).astype(BF)

    def put(p, carry):
        spread[p] = total
        return carry

    lax.fori_loop(0, 64, put, 0, unroll=8)


def finish(core_of_first, source, outs, wide, sems):
    core = lax.axis_index("core")
    parts = 4
    rows = ROWS // parts
    for q in range(parts):
        at = pl.ds(q * rows, rows)
        wide[at, :] = source[at, :].astype(F32)
        for out, there in zip(outs, (core == core_of_first, core != core_of_first)):

            @pl.when(there)
            def _():
                pltpu.make_async_copy(wide.at[at], out.at[at], sems.at[q]).start()

    for q in range(parts):
        at = pl.ds(q * rows, rows)
        pltpu.make_async_copy(wide.at[at], outs[0].at[at], sems.at[q]).wait()


def finish_own_kernel(own, first_grad, second_grad, wide, sems):
    finish(0, own, (first_grad, second_grad), wide, sems)


def finish_other_kernel(other, first_in, second_in, first_grad, second_grad, wide, sems):
    finish(1, other, (first_grad, second_grad), wide, sems)


def send_shapes(fields):
    return tuple(jax.ShapeDtypeStruct((fields * w * 64, 128), BF) for w in (2, 2, 2, 2, 4))


def call(kernel, outs, ins, specs, scratch, limit, flops=0, nbytes=0, out_specs=VMEM, aliases={}):
    many = isinstance(outs, tuple)
    ins = [
        pltpu.with_memory_space_constraint(a, pltpu.HBM) if spec is HBM else a
        for a, spec in zip(ins, specs)
    ]
    return pl.pallas_call(
        kernel,
        out_shape=outs,
        in_specs=specs,
        out_specs=tuple(out_specs for _ in outs) if many else out_specs,
        scratch_shapes=scratch,
        input_output_aliases=aliases,
        compiler_params=pltpu.CompilerParams(vmem_limit_bytes=limit << 20),
        cost_estimate=pl.CostEstimate(flops=flops, bytes_accessed=nbytes, transcendentals=0),
    )(*ins)


def in_vmem(shape, dtype):
    return pltpu.VMEM(shape, dtype)


def step(voxels, occupied, neighbours, first_weight, second_weight, cotangent):
    field = pltpu.VMEM((4, 512, 128), F32)
    raw = pltpu.VMEM((1, 4, 512, 128), BF)
    links = pltpu.SMEM((1, 4, 6), jnp.int32)
    flags = pltpu.SMEM((1, 4), jnp.int32)
    weights = pltpu.VMEM((27, 128, 128), BF)
    sides = [pltpu.VMEM((4, 2, 64, 128), F32)] * 3
    padded = [pltpu.VMEM((3, 4, 10, 80, 128), BF), pltpu.VMEM((3, 4, 10, 64, 128), BF)]
    pairs = pltpu.VMEM((4608, 256), BF)
    turned = pltpu.VMEM((128, 2048), BF)
    sems = pltpu.SemaphoreType.DMA((5,))
    blocks = jax.ShapeDtypeStruct((4, 512, 128), BF)
    terms_shape = jax.ShapeDtypeStruct((ROWS, 128), F32)

    sent = call(
        first_faces_kernel,
        send_shapes(2),
        (voxels, cotangent, neighbours),
        [HBM] * 3,
        [field, field, raw, raw, links, sems],
        10,
        nbytes=2 << 20,
    )
    got = exchange(sent)
    prepared = call(
        prepare_kernel,
        (in_vmem((4, 512, 128), F32),) * 2 + (in_vmem((4608, 256), BF),) * 2,
        (voxels, cotangent, occupied, first_weight, second_weight),
        [HBM] * 5,
        [raw, raw, weights, weights, flags, sems],
        8,
        flops=1 << 20,
        nbytes=8 << 20,
    )
    hidden, own, other = call(
        main_kernel,
        (blocks, terms_shape, jax.ShapeDtypeStruct((ROWS, 128), BF)),
        tuple(prepared) + (neighbours, occupied) + got,
        [VMEM] * 4 + [HBM] * 2 + [VMEM] * 5,
        sides + sides + padded + padded + [field, turned, turned, links, flags, sems],
        26,
        flops=8 << 30,
        nbytes=8 << 20,
    )
    other = lax.ppermute(other, "core", PARTNER)
    chunks = jax.ShapeDtypeStruct((64 * CHUNK, 128), BF)
    terms = call(
        pair_kernel,
        chunks,
        (own, other),
        [VMEM] * 2,
        [pltpu.VMEM((64 * CHUNK, 128), BF), pltpu.SemaphoreType.DMA((8,))],
        4,
        nbytes=4 << 20,
        out_specs=HBM,
    )
    parts = lax.all_to_all(
        terms.reshape(64, CHUNK, 128), PEERS, split_axis=0, concat_axis=0, tiled=True
    )
    sent = call(
        hidden_faces_kernel,
        send_shapes(1),
        (hidden, neighbours),
        [VMEM, HBM],
        [field, links, sems],
        6,
        nbytes=1 << 20,
    )
    got = exchange(sent)
    spread = call(
        sum_kernel,
        jax.ShapeDtypeStruct((64, CHUNK, 128), BF),
        (parts,) + tuple(sent),
        [VMEM] + [ANY] * 5,
        [],
        6,
        nbytes=2 << 20,
    )
    mine = lax.all_to_all(spread, PEERS, split_axis=0, concat_axis=0, tiled=True)
    output = call(
        last_kernel,
        jax.ShapeDtypeStruct((1, 4, 512, 128), BF),
        (prepared[0], hidden, neighbours, occupied, second_weight) + got,
        [VMEM] * 2 + [HBM] * 3 + [VMEM] * 5,
        [field] + sides + padded + [pairs, weights, links, flags, sems],
        20,
        flops=3 << 30,
        nbytes=4 << 20,
    )
    mine, output = lax.optimization_barrier((mine, output))
    mine = mine.reshape(64 * CHUNK, 128)
    theirs = lax.ppermute(mine, "core", PARTNER)
    wide = pltpu.VMEM((ROWS, 128), F32)
    grads = call(
        finish_own_kernel, (terms_shape, terms_shape), (mine,), [VMEM], [wide, sems], 4, nbytes=3 << 20, out_specs=HBM
    )
    first_grad, second_grad = call(
        finish_other_kernel,
        (terms_shape, terms_shape),
        (theirs,) + tuple(grads),
        [VMEM, HBM, HBM],
        [wide, sems],
        4,
        nbytes=3 << 20,
        out_specs=HBM,
        aliases={1: 0, 2: 1},
    )
    return output, first_grad.reshape(27, 128, 128), second_grad.reshape(27, 128, 128)


def solution(mesh):
    mesh = jax.sharding.Mesh(mesh.devices.reshape(4, 4, 2, 4), ("z", "x", "core", "rep"))
    placed = (
        P("rep", SPACE, None, None),
        P("rep", SPACE),
        P("rep", SPACE, None),
        P(),
        P(),
        P("rep", SPACE, None, None),
    )
    return jax.shard_map(
        step,
        mesh=mesh,
        in_specs=placed,
        out_specs=(P("rep", SPACE, None, None), P(), P()),
        check_vma=False,
    )
```
